512 devices in a mesh: node: 128 (over z, y, core), feat: 4 (over x).
Axes of the slice: x: 4, y: 8, z: 8, core: 2. Of those that a mesh axis runs over, the one named last changes fastest.
Arguments:
- embed: bfloat16 [256, 131072], P('feat', 'node'), may hold values from -6 to 6
- tile_weight: bfloat16 [128, 135, 128, 128], P('node'), may hold values from -0.125 to 0.125
- tile_rows: int32 [128, 135], P('node'), may hold values from 0 to 7
- tile_cols: int32 [128, 135], P('node'), may hold values from 0 to 135, as said below
- send_rows: int32 [128, 128], P('node'), may hold values from 0 to 7
- src_local: int32 [65536], P('node'), may hold values from 0 to 1023
- dst_owner: int32 [65536, 1], P('node'), may hold values from 0 to 127; in each aligned block of 512 rows (0 to 511, 512 to 1023, ...) at most 8 rows name the same one
- dst_local: int32 [65536], P('node'), may hold values from 0 to 1023
- w_in: bfloat16 [256, 1024], P('feat'), may hold values from -0.375 to 0.375
- b_in: float32 [1024], replicated, may hold values from -4 to 4
- w_out: float32 [1024], replicated, may hold values from -0.1875 to 0.1875
Outputs:
- propagated: bfloat16 [256, 131072], P('feat', 'node')
- scores: float32 [65536], P('node')
The draws below stay inside these ranges and needn't reach their ends.
Inputs may be any that keep to these rules, and one draw needn't show every extreme that they name: In each part, the entries of tile_cols below 8 are the numbers 0 to 7 once each, and tile_rows equals tile_cols at those tiles; the other 127 entries are 8 + p for every part p other than the part itself, once each. `dst_owner`: among the 512 queries of one part, at most 8 have the same destination part, and exactly 8 do for some destination part.
All inputs are finite; a program needn't handle non-finite values.
Results may differ from the reference program's by a relative error of at most 0.015.
Values may be sent and summed in bfloat16 or wider, within the bound.
A program may use at most 64 MiB of HBM per device.

```python
import math
import jax
import jax.numpy as jnp
import numpy as np
from jax import lax

D = 256
HID = 1024
B = 128
HOPS = 2
NODE_DEV = 1024
Q_DEV = 512
PARTS_SIZE = 128
RB = 8
HALF = 127
TILES = 135
CAP = 8
NODES = 131072
QUERIES = 65536


def tile_links(key):
    base_key = jax.random.fold_in(key, 11)

    def per_part(part_index):
        key_peer, key_row, key_order = jax.random.split(jax.random.fold_in(base_key, part_index), 3)
        others = (part_index + 1 + jax.random.permutation(key_peer, PARTS_SIZE - 1)) % PARTS_SIZE
        row_list = jnp.concatenate([jnp.arange(RB, dtype=jnp.int32), jax.random.randint(key_row, (HALF,), 0, RB, dtype=jnp.int32)])
        col_list = jnp.concatenate([jnp.arange(RB, dtype=jnp.int32), (RB + others[:HALF]).astype(jnp.int32)])
        order_list = jax.random.permutation(key_order, TILES)
        return (row_list[order_list], col_list[order_list])
    return jax.vmap(per_part)(jnp.arange(PARTS_SIZE, dtype=jnp.int32))


def draw_tile_rows(key, part):
    return tile_links(key)[0].astype(jnp.int32)


def draw_tile_cols(key, part):
    return tile_links(key)[1].astype(jnp.int32)


def touch_ends(result, stream_key, smallest, high):
    longest = result.shape.index(max(result.shape))
    spots = []
    for shift in (0, 1):
        where = [jax.random.randint(jax.random.fold_in(stream_key, axis), (), 0, length) for axis, length in enumerate(result.shape)]
        where[longest] = (where[longest] + shift) % result.shape[longest]
        spots.append(tuple(where))
    return result.at[spots[0]].set(smallest).at[spots[1]].set(high)


def levels(stream_key, shape, shards, least, largest):
    def one(position, blocks):
        steps = jax.random.uniform(jax.random.fold_in(jax.random.fold_in(stream_key, 6), position), (blocks,), jnp.float32, least / len(shards), largest / len(shards))
        return jnp.repeat(jnp.exp(steps), shape[position] // blocks).reshape((-1,) + (1,) * (len(shape) - position - 1))

    factor_of = one(*shards[0])
    for cut in shards[1:]:
        factor_of = factor_of * one(*cut)
    return factor_of


def assign_block(key, own, number, rows, amount, top, reach, skew):
    sequence = jax.random.permutation(key, amount)
    heavy_load, common = portions_of(amount, rows * top, reach, skew, True), portions_of(amount, rows * top, reach, skew, False)
    places = jnp.arange(amount)

    def named(tallies, offset_by):
        used = int((tallies > 0).sum())
        fixed = max(1, used // 4)
        moved = fixed + (places - fixed + offset_by * (used - fixed)) % max(1, amount - fixed)
        return jnp.zeros((amount,), jnp.int32).at[sequence[jnp.where(places < fixed, places, moved)]].set(jnp.asarray(tallies, jnp.int32))

    tallies = jnp.where(number % 4 == 0, named(heavy_load, number // 4), named(common, number - number // 4 - 1))
    mixed = jax.random.permutation(jax.random.fold_in(own, 3), amount)
    source_of, receiver = mixed[0:amount // 2 * 2:2], mixed[1:amount // 2 * 2:2]
    room = jnp.minimum(tallies[source_of] - 1, reach - tallies[receiver]) // 2
    room = jnp.where((source_of == sequence[0]) | (receiver == sequence[0]) | (tallies[receiver] == 0), 0, jnp.maximum(room, 0))
    moved = jax.random.randint(jax.random.fold_in(own, 4), (amount // 2,), 0, 1 << 20) % (room + 1)
    tallies = tallies.at[source_of].add(-moved).at[receiver].add(moved)
    members = jnp.searchsorted(jnp.cumsum(tallies), jnp.arange(rows * top), side="right").astype(jnp.int32)
    listing = members.reshape(top, rows).T
    listing = listing[jax.random.permutation(jax.random.fold_in(own, 1), rows)]
    offset_by = jax.random.randint(jax.random.fold_in(own, 2), (rows, 1), 0, top)
    return jnp.take_along_axis(listing, (jnp.arange(top)[None, :] + offset_by) % top, axis=1)


def portions_of(amount, total, most, skew, full):
    loads = [(1 << 20) // math.isqrt(standing ** skew) + 1 for standing in range(1, amount + 1)]
    largest = most if full else min(most, max(-(-total // amount), total * loads[0] // sum(loads)))
    least = 1 if total - largest >= amount - 1 else 0
    holding, rest = [largest] + [least] * (amount - 1), total - largest - least * (amount - 1)
    while rest > 0:
        movable = [i for i in range(1, amount) if holding[i] < largest] or [i for i in range(1, amount) if holding[i] < most]
        mass, budget = sum([loads[i] for i in movable]), rest
        for i in movable:
            extra = min(most - holding[i], max(1, budget * loads[i] // mass), rest)
            holding[i] = holding[i] + extra
            rest = rest - extra
    return np.array(holding)


def centred(key, extent, scale, bound, cuts=(), kind=jnp.bfloat16):
    drawn = jax.random.normal(key, extent, jnp.float32) * scale
    if len(cuts) > 0:
        drawn = levels(key, extent, cuts, -0.22, 0.18) * drawn
    return jnp.clip(drawn, min=-bound, max=bound).astype(kind)


def setup_inputs(seed: int = 0) -> dict:
    seeds = jax.random.split(jax.random.key(seed), 12)
    embed = centred(seeds[0], (D, NODES), 1.0, 6.0, ((0, 4), (1, 128)))
    tile_weight = centred(seeds[1], (PARTS_SIZE, TILES, B, B), (B * TILES // RB) ** -0.5, 0.125, ((0, 128),))
    tile_rows = draw_tile_rows(jax.random.fold_in(seeds[11], 71), 0)
    tile_cols = draw_tile_cols(jax.random.fold_in(seeds[11], 71), 0)
    send_rows = touch_ends(jax.random.randint(seeds[4], (PARTS_SIZE, PARTS_SIZE), 0, RB), jax.random.fold_in(seeds[4], 1), 0, RB - 1).astype(jnp.int32)
    src_local = touch_ends(jax.random.randint(seeds[5], (QUERIES,), 0, NODE_DEV), jax.random.fold_in(seeds[5], 1), 0, NODE_DEV - 1).astype(jnp.int32)
    dst_owner_keys = jax.random.split(jax.random.fold_in(seeds[6], 1), QUERIES // Q_DEV)
    dst_owner_turns = jax.random.permutation(jax.random.fold_in(seeds[6], 3), QUERIES // Q_DEV)
    dst_owner = jax.vmap(lambda own, number: assign_block(jax.random.fold_in(seeds[6], 2), own, number, Q_DEV, PARTS_SIZE, 1, CAP, 1))(dst_owner_keys, dst_owner_turns).reshape((QUERIES, 1))
    dst_local = touch_ends(jax.random.randint(seeds[7], (QUERIES,), 0, NODE_DEV), jax.random.fold_in(seeds[7], 1), 0, NODE_DEV - 1).astype(jnp.int32)
    w_in = centred(seeds[8], (D, HID), D ** -0.5, 0.375, ((0, 4),))
    b_in = centred(seeds[9], (HID,), 1.0, 4.0, (), jnp.float32)
    w_out = centred(seeds[10], (HID,), HID ** -0.5, 0.1875, (), jnp.float32)
    return {"embed": embed, "tile_weight": tile_weight, "tile_rows": tile_rows, "tile_cols": tile_cols, "send_rows": send_rows, "src_local": src_local, "dst_owner": dst_owner, "dst_local": dst_local, "w_in": w_in, "b_in": b_in, "w_out": w_out}


TELEPORT = 0.1


def propagate(current, initial, tile_weight, tile_rows, tile_cols, send_rows):
    blocked = current.reshape(PARTS_SIZE * RB, B, D)

    def per_part(owner_part):
        tile_col = tile_cols[owner_part]
        peer_part = jnp.clip(tile_col - RB, 0, PARTS_SIZE - 1).astype(jnp.int32)
        remote = (peer_part * RB + send_rows[peer_part, owner_part]).astype(jnp.int32)
        source = jnp.where(tile_col < RB, owner_part * RB + tile_col, remote).astype(jnp.int32)
        picked = blocked[source].astype(jnp.float32)
        products = jnp.einsum("tij,tjd->tid", tile_weight[owner_part].astype(jnp.float32), picked)
        return jax.ops.segment_sum(products, tile_rows[owner_part], num_segments=RB)

    summed = lax.map(per_part, jnp.arange(PARTS_SIZE, dtype=jnp.int32)).reshape(NODES, D)
    return ((1.0 - TELEPORT) * summed + TELEPORT * initial).astype(jnp.bfloat16)


def reference(embed, tile_weight, tile_rows, tile_cols, send_rows, src_local, dst_owner, dst_local, w_in, b_in, w_out):
    initial_rows = embed.T
    initial = initial_rows.astype(jnp.float32)
    current = initial_rows
    for hop_index in range(HOPS):
        current = propagate(current, initial, tile_weight, tile_rows, tile_cols, send_rows)
    query_part = jnp.arange(QUERIES, dtype=jnp.int32) // Q_DEV
    source_node = (query_part * NODE_DEV + src_local).astype(jnp.int32)
    target_node = (dst_owner[:, 0] * NODE_DEV + dst_local).astype(jnp.int32)
    hadamard = (current[source_node].astype(jnp.float32) * current[target_node].astype(jnp.float32)).astype(jnp.bfloat16)
    hidden = jnp.dot(hadamard, w_in, preferred_element_type=jnp.float32)
    active = jnp.maximum(hidden + b_in, 0.0)
    scores = jnp.dot(active, w_out, precision=lax.Precision.HIGHEST)
    return current.T, scores
```

```python
import jax
import jax.numpy as jnp
from jax import lax
from jax.experimental import pallas as pl
from jax.experimental.pallas import tpu as pltpu
from jax.sharding import PartitionSpec as P

Z, Y, C, X = 8, 8, 2, 4
RB, B, CAP = 8, 128, 8
HOPS = 2
TELEPORT = 0.1
MESH = pl.DeviceIdType.MESH
F32, BF16, I32 = jnp.float32, jnp.bfloat16, jnp.int32


def dot(left, right, left_dim, right_dim):
    return lax.dot_general(
        left, right, (((left_dim,), (right_dim,)), ((), ())), preferred_element_type=F32
    )


def iota(shape, dim):
    return lax.broadcasted_iota(I32, shape, dim)


def kernel(
    embed, weight_hbm, tile_rows, tile_cols, send_rows, src_local, dst_owner, dst_local, w_in, b_in, w_out,
    out, scores,
    cur0, cur1, cur2, gz0, gy0, gz1, gy1, sa0, sb0, sa1, sb1, ra0, rb0, ra1, rb1,
    weight, total, cols, table, table_s, sr_own, srz, sry, srz_s, sry_s,
    req, reqz, reqm, reqy, pick, pick_src, pick_slot, reply, mid, got,
    wfull, wt, bcol, ocol, had, hadfull,
    local_sem, sz_send, sz_recv, sy_send, sy_recv, a_send, a_recv, b_send, b_recv,
    qz_send, qz_recv, qy_send, qy_recv, pa_send, pa_recv, pb_send, pb_recv,
    rz_send, rz_recv, ry_send, ry_recv, wx_send, wx_recv, hx_send, hx_recv,
):
    parts = Z * Y * C
    yc, zc = Y * C, Z * C
    queries = src_local.shape[1]
    nodes = embed.shape[1]
    half = embed.shape[0] // 2
    me, xf = lax.axis_index("node"), lax.axis_index("feat")
    z, j = me // yc, me % yc
    y, c = j // C, j % C
    k = z * C + c

    def at_a(jd):
        return (z * yc + jd, xf)

    def at_b(kd):
        return (((kd // C) * Y + y) * C + kd % C, xf)

    def at_z(zd):
        return ((zd * Y + y) * C + c, xf)

    def at_y(yd):
        return ((z * Y + yd) * C + c, xf)

    def at_x(xd):
        return (me, xd)

    def push(src, dst, send, recv, device):
        return pltpu.make_async_remote_copy(
            src_ref=src, dst_ref=dst, send_sem=send, recv_sem=recv, device_id=device, device_id_type=MESH
        )

    def each(lo, hi, body):
        def step(i, carry):
            body(i)
            return carry
        lax.fori_loop(lo, hi, step, 0)

    def zigzag(i, n):
        return jnp.where(i % 2 == 1, (i + 1) // 2, n - i // 2)

    barrier = pltpu.get_barrier_semaphore()

    def greet(device):
        pl.semaphore_signal(barrier, inc=1, device_id=device, device_id_type=MESH)

    each(1, yc, lambda e: greet(at_a((j + e) % yc)))
    each(1, zc, lambda e: greet(at_b((k + e) % zc)))
    each(1, X, lambda e: greet(at_x((xf + e) % X)))

    fetch = pltpu.make_async_copy(weight_hbm.at[0], weight, local_sem.at[0])
    fetch.start()
    for r in range(RB):
        for h in range(2):
            cur0[h, r] = embed[h * half:(h + 1) * half, r * B:(r + 1) * B]
    sr_own[...] = send_rows[...].reshape(1, parts)

    pl.semaphore_wait(barrier, yc - 1 + zc - 1 + X - 1)

    def share(hop, cur, gz, gy):
        def go_z(d):
            zd = (z + d) % Z
            push(cur.at[0], gz.at[z], sz_send.at[hop, d], sz_recv.at[hop, z], at_z(zd)).start()
        def go_y(d):
            yd = (y + d) % Y
            push(cur.at[1], gy.at[y], sy_send.at[hop, d], sy_recv.at[hop, y], at_y(yd)).start()
        each(1, Z, lambda i: go_z(zigzag(i, Z)))
        each(1, Y, lambda i: go_y(zigzag(i, Y)))
        gz[z] = cur[0]
        gy[y] = cur[1]

    def shared(hop, cur, gz, gy):
        def end_z(d):
            s = (z + d) % Z
            push(cur.at[0], gz.at[s], sz_send.at[hop, d], sz_recv.at[hop, s], at_z(s)).wait_recv()
        def end_y(d):
            s = (y + d) % Y
            push(cur.at[1], gy.at[s], sy_send.at[hop, d], sy_recv.at[hop, s], at_y(s)).wait_recv()
        each(1, Z, end_z)
        each(1, Y, end_y)

    def deal(hop, gz, gy, sa, sb, ra, rb):
        def fill_a(jd, dst):
            for s in range(Z):
                dst[jd, s] = gz[s, srz_s[s, 0, z * yc + jd]]
        def fill_b(kd, dst):
            for s in range(Y):
                dst[kd, s] = gy[s, sry_s[s, 0, ((kd // C) * Y + y) * C + kd % C]]
        def go_a(i):
            jd = (j + zigzag(i, yc)) % yc
            fill_a(jd, sa)
            push(sa.at[jd], ra.at[j], a_send.at[hop, jd], a_recv.at[hop, j], at_a(jd)).start()
        def go_b(i):
            kd = (k + zigzag(i, zc)) % zc
            fill_b(kd, sb)
            push(sb.at[kd], rb.at[k], b_send.at[hop, kd], b_recv.at[hop, k], at_b(kd)).start()
        each(1, yc, go_a)
        each(1, zc, go_b)
        fill_a(j, ra)
        fill_b(k, rb)

    def dealt(hop, sa, sb, ra, rb):
        def end_a(e):
            s = (j + e) % yc
            push(sa.at[s], ra.at[s], a_send.at[hop, s], a_recv.at[hop, s], at_a(s)).wait_recv()
        def end_b(e):
            s = (k + e) % zc
            push(sb.at[s], rb.at[s], b_send.at[hop, s], b_recv.at[hop, s], at_b(s)).wait_recv()
        each(1, yc, end_a)
        each(1, zc, end_b)

    def combine(cur, ra, rb, nxt):
        def term(s, block):
            product = dot(block, weight[table_s[0, s]], 1, 1)
            total[s] = product + total[table_s[1, s]]
        def column(jd):
            yd, cd = jd // C, jd % C
            for s in range(Z):
                term(jd * Z + s, jnp.concatenate([ra[jd, s], rb[s * C + cd, yd]], axis=0))
        total[parts + RB] = jnp.zeros(total.shape[1:], F32)
        each(0, yc, column)
        for r in range(RB):
            term(parts + r, jnp.concatenate([cur[0, r], cur[1, r]], axis=0))
        for r in range(RB):
            first = jnp.concatenate([cur0[0, r], cur0[1, r]], axis=0).astype(F32)
            new = ((1.0 - TELEPORT) * total[parts + r] + TELEPORT * first).astype(BF16)
            nxt[0, r] = new[:half]
            nxt[1, r] = new[half:]

    share(0, cur0, gz0, gy0)

    def rows_z(d):
        push(sr_own, srz.at[z], rz_send.at[d], rz_recv.at[z], at_z((z + d) % Z)).start()
    def rows_y(d):
        push(sr_own, sry.at[y], ry_send.at[d], ry_recv.at[y], at_y((y + d) % Y)).start()
    each(1, Z, rows_z)
    each(1, Y, rows_y)
    srz[z] = sr_own[...]
    sry[y] = sr_own[...]
    each(1, X, lambda d: push(
        w_in, wfull.at[xf], wx_send.at[d], wx_recv.at[xf], at_x((xf + d) % X)).start())
    wfull[xf] = w_in[...]

    slots = cols.shape[1]
    cols[...] = jnp.full(cols.shape, -1, I32)
    tiles = tile_cols.shape[1]
    cols[0:1, 0:tiles] = tile_cols[...]
    cols[8:9, 0:tiles] = tile_rows[...]
    col = cols[0:1, :]
    peer = col - RB
    peer_slot = (peer % yc) * Z + peer // yc
    slot_of = jnp.where(col < 0, -1, jnp.where(col < RB, parts + col, peer_slot))
    hit = (iota((slots, slots), 0) == slot_of).astype(F32).astype(BF16)
    kind = iota((8, slots), 0)
    facts = jnp.where(kind == 0, iota((8, slots), 1), jnp.where(kind == 1, cols[8:9, :], 1))
    found = dot(facts.astype(F32).astype(BF16), hit, 1, 1)
    row_of = jnp.where(found[2:3, :] > 0.5, found[1:2, :], -1.0)
    row_hit = (iota((128, slots), 0).astype(F32) == row_of).astype(F32).astype(BF16)
    same = dot(row_hit, row_hit, 0, 0)
    before = jnp.where(
        (same > 0.5) & (iota((slots, slots), 0) < iota((slots, slots), 1)), iota((slots, slots), 0).astype(F32), -1.0
    )
    last = jnp.max(before, axis=0, keepdims=True)
    table[0:1, :] = jnp.clip(found[0:1, :].astype(I32), 0, tiles - 1)
    table[1:2, :] = jnp.clip(jnp.where(last < 0.0, float(parts + RB), last).astype(I32), 0, parts + RB)
    to_smem = pltpu.make_async_copy(table, table_s, local_sem.at[1])
    to_smem.start()

    owner = dst_owner[...]
    owns = (iota((parts, queries), 0) == owner).astype(F32).astype(BF16)
    alike = dot(owns, owns, 0, 0)
    earlier = iota((queries, queries), 0) < iota((queries, queries), 1)
    rank = jnp.sum(jnp.where(earlier, alike, 0.0), axis=0, keepdims=True).astype(I32)
    place = iota((128, queries), 0) == rank
    high, low = dst_local[...] // 32, dst_local[...] % 32
    ask_high = dot(owns, jnp.where(place, high, 0).astype(F32).astype(BF16), 1, 1)
    ask_low = dot(owns, jnp.where(place, low, 0).astype(F32).astype(BF16), 1, 1)
    req[...] = (ask_high * 32.0 + ask_low).astype(I32).reshape(Z, yc, 128)
    def ask_z(d):
        zd = (z + d) % Z
        push(req.at[zd], reqz.at[z], qz_send.at[d], qz_recv.at[z], at_z(zd)).start()
    each(1, Z, ask_z)
    reqz[z] = req[z]
    slot = owner * CAP + rank
    pick_slot[...] = (iota(pick_slot.shape, 0) == slot).astype(F32).astype(BF16)
    pick_src[...] = (iota(pick_src.shape, 0) == src_local[...]).astype(F32).astype(BF16)

    def rows_z_end(d):
        s = (z + d) % Z
        push(sr_own, srz.at[s], rz_send.at[d], rz_recv.at[s], at_z(s)).wait_recv()
    def rows_y_end(d):
        s = (y + d) % Y
        push(sr_own, sry.at[s], ry_send.at[d], ry_recv.at[s], at_y(s)).wait_recv()
    each(1, Z, rows_z_end)
    each(1, Y, rows_y_end)
    rows_copies = [
        pltpu.make_async_copy(srz, srz_s, local_sem.at[2]),
        pltpu.make_async_copy(sry, sry_s, local_sem.at[3]),
    ]
    for copy in rows_copies:
        copy.start()
    for copy in rows_copies:
        copy.wait()
    shared(0, cur0, gz0, gy0)
    deal(0, gz0, gy0, sa0, sb0, ra0, rb0)

    def ask_z_end(d):
        s = (z + d) % Z
        push(req.at[s], reqz.at[s], qz_send.at[d], qz_recv.at[s], at_z(s)).wait_recv()
    each(1, Z, ask_z_end)
    for jd in range(yc):
        reqm[jd] = jnp.concatenate([reqz[s, jd:jd + 1, :] for s in range(Z)], axis=0)
    def ask_y(e):
        jd = (j + e) % yc
        push(reqm.at[jd], reqy.at[j], qy_send.at[e], qy_recv.at[j], at_a(jd)).start()
    each(1, yc, ask_y)
    reqy[j] = reqm[j]

    def w_end(d):
        s = (xf + d) % X
        push(w_in, wfull.at[s], wx_send.at[d], wx_recv.at[s], at_x(s)).wait_recv()
    each(1, X, w_end)
    hidden_units = w_in.shape[1]
    channels = w_in.shape[0]
    for n in range(hidden_units // 128):
        lanes = slice(n * 128, (n + 1) * 128)
        whole = jnp.concatenate([wfull[s, :, lanes] for s in range(X)], axis=0)
        wt[lanes, :] = whole.astype(F32).T.astype(BF16)
        bcol[lanes, :] = jnp.broadcast_to(b_in[0:1, lanes], (128, 128)).T
        ocol[lanes, :] = jnp.broadcast_to(w_out[0:1, lanes], (128, 128)).T

    to_smem.wait()
    fetch.wait()
    dealt(0, sa0, sb0, ra0, rb0)
    combine(cur0, ra0, rb0, cur1)

    share(1, cur1, gz1, gy1)
    shared(1, cur1, gz1, gy1)
    deal(1, gz1, gy1, sa1, sb1, ra1, rb1)

    def ask_y_end(e):
        s = (j + e) % yc
        push(reqm.at[s], reqy.at[s], qy_send.at[e], qy_recv.at[s], at_a(s)).wait_recv()
    each(1, yc, ask_y_end)
    asked = reqy[...].reshape(yc * Z, 128)
    for n in range(CAP):
        pick[n] = (iota((parts, nodes), 1) == asked[:, n:n + 1]).astype(F32).astype(BF16)

    dealt(1, sa1, sb1, ra1, rb1)
    combine(cur1, ra1, rb1, cur2)
    for r in range(RB):
        for h in range(2):
            out[h * half:(h + 1) * half, r * B:(r + 1) * B] = cur2[h, r]

    final = out[...]
    def reply_rows(n):
        rows = dot(pick[n], final, 1, 1)
        return rows.reshape(yc, Z, 1, channels)
    reply[...] = jnp.concatenate([reply_rows(n) for n in range(CAP)], axis=2).astype(BF16)
    def reply_a(i):
        jd = (j + i) % yc
        push(reply.at[jd], mid.at[j], pa_send.at[i], pa_recv.at[j], at_a(jd)).start()
    each(1, yc, reply_a)
    mid[j] = reply[j]
    source = dot(final, pick_src[...], 1, 0)
    def reply_a_end(e):
        s = (j + e) % yc
        push(reply.at[s], mid.at[s], pa_send.at[e], pa_recv.at[s], at_a(s)).wait_recv()
    each(1, yc, reply_a_end)
    def reply_z(d):
        zd = (z + d) % Z
        push(mid.at[:, zd], got.at[z], pb_send.at[d], pb_recv.at[z], at_z(zd)).start()
    each(1, Z, reply_z)
    got[z] = mid[:, z]
    def reply_z_end(d):
        s = (z + d) % Z
        push(mid.at[:, s], got.at[s], pb_send.at[d], pb_recv.at[s], at_z(s)).wait_recv()
    each(1, Z, reply_z_end)
    target = dot(got[...].reshape(parts * CAP, channels), pick_slot[...], 0, 0)
    had[...] = (source * target).astype(BF16)
    def had_x(d):
        push(had, hadfull.at[xf], hx_send.at[d], hx_recv.at[xf], at_x((xf + d) % X)).start()
    each(1, X, had_x)
    hadfull[xf] = had[...]
    def had_x_end(d):
        s = (xf + d) % X
        push(had, hadfull.at[s], hx_send.at[d], hx_recv.at[s], at_x(s)).wait_recv()
    each(1, X, had_x_end)
    everything = hadfull[...].reshape(X * channels, queries)
    score = jnp.zeros((8, queries), F32)
    for n in range(hidden_units // 128):
        lanes = slice(n * 128, (n + 1) * 128)
        hidden = dot(wt[lanes, :], everything, 1, 0)
        bias, gain = bcol[lanes, :], ocol[lanes, :]
        if queries > 128:
            bias, gain = (jnp.concatenate([v] * (queries // 128), axis=1) for v in (bias, gain))
        else:
            bias, gain = bias[:, :queries], gain[:, :queries]
        active = jnp.maximum(hidden + bias, 0.0) * gain
        score = score + jnp.sum(active.reshape(16, 8, queries), axis=0)
    scores[...] = jnp.sum(score, axis=0, keepdims=True)

    for hop, cur, gz, gy, sa, sb, ra, rb in (
        (0, cur0, gz0, gy0, sa0, sb0, ra0, rb0), (1, cur1, gz1, gy1, sa1, sb1, ra1, rb1)
    ):
        each(1, Z, lambda d: push(
            cur.at[0], gz.at[z], sz_send.at[hop, d], sz_recv.at[hop, z], at_z((z + d) % Z)).wait_send())
        each(1, Y, lambda d: push(
            cur.at[1], gy.at[y], sy_send.at[hop, d], sy_recv.at[hop, y], at_y((y + d) % Y)).wait_send())
        def left_a(e):
            jd = (j + e) % yc
            push(sa.at[jd], ra.at[j], a_send.at[hop, jd], a_recv.at[hop, j], at_a(jd)).wait_send()
        def left_b(e):
            kd = (k + e) % zc
            push(sb.at[kd], rb.at[k], b_send.at[hop, kd], b_recv.at[hop, k], at_b(kd)).wait_send()
        each(1, yc, left_a)
        each(1, zc, left_b)
    def left_z(d):
        zd = (z + d) % Z
        push(sr_own, srz.at[z], rz_send.at[d], rz_recv.at[z], at_z(zd)).wait_send()
        push(req.at[zd], reqz.at[z], qz_send.at[d], qz_recv.at[z], at_z(zd)).wait_send()
        push(mid.at[:, zd], got.at[z], pb_send.at[d], pb_recv.at[z], at_z(zd)).wait_send()
    each(1, Z, left_z)
    each(1, Y, lambda d: push(
        sr_own, sry.at[y], ry_send.at[d], ry_recv.at[y], at_y((y + d) % Y)).wait_send())
    def left_y(e):
        jd = (j + e) % yc
        push(reqm.at[jd], reqy.at[j], qy_send.at[e], qy_recv.at[j], at_a(jd)).wait_send()
        push(reply.at[jd], mid.at[j], pa_send.at[e], pa_recv.at[j], at_a(jd)).wait_send()
    each(1, yc, left_y)
    def left_x(d):
        xd = (xf + d) % X
        push(w_in, wfull.at[xf], wx_send.at[d], wx_recv.at[xf], at_x(xd)).wait_send()
        push(had, hadfull.at[xf], hx_send.at[d], hx_recv.at[xf], at_x(xd)).wait_send()
    each(1, X, left_x)


def shards(
    embed, tile_weight, tile_rows, tile_cols, send_rows, src_local, dst_owner, dst_local, w_in, b_in, w_out
):
    parts, yc, zc = Z * Y * C, Y * C, Z * C
    channels, nodes = embed.shape
    half = channels // 2
    queries, hidden = src_local.shape[0], w_in.shape[1]
    tiles = tile_rows.shape[1]
    slots = 256
    V, S, D = pltpu.VMEM, pltpu.SMEM, pltpu.SemaphoreType.DMA
    cur = [V((2, RB, half, B), BF16)] * 3
    near = [V((n, RB, half, B), BF16) for n in (Z, Y, Z, Y)]
    deal = [V((n, m, half, B), BF16) for n, m in ((yc, Z), (zc, Y))]
    scratch = cur + near + deal * 4 + [
        V((tiles, B, B), BF16), V((parts + RB + 1, channels, B), F32),
        V((16, slots), I32), V((8, slots), I32), S((8, slots), I32),
        V((1, parts), I32), V((Z, 1, parts), I32), V((Y, 1, parts), I32), S((Z, 1, parts), I32), S((Y, 1, parts), I32),
        V((Z, yc, 128), I32), V((Z, yc, 128), I32), V((yc, Z, 128), I32), V((yc, Z, 128), I32),
        V((CAP, parts, nodes), BF16), V((nodes, queries), BF16), V((parts * CAP, queries), BF16),
        V((yc, Z, CAP, channels), BF16), V((yc, Z, CAP, channels), BF16), V((Z, yc, CAP, channels), BF16),
        V((X, channels, hidden), BF16), V((hidden, X * channels), BF16), V((hidden, 128), F32), V((hidden, 128), F32),
        V((channels, queries), BF16), V((X, channels, queries), BF16),
        D((4,)), D((HOPS, Z)), D((HOPS, Z)), D((HOPS, Y)), D((HOPS, Y)),
        D((HOPS, yc)), D((HOPS, yc)), D((HOPS, zc)), D((HOPS, zc)),
        D((Z,)), D((Z,)), D((yc,)), D((yc,)), D((yc,)), D((yc,)), D((Z,)), D((Z,)),
        D((Z,)), D((Z,)), D((Y,)), D((Y,)), D((X,)), D((X,)), D((X,)), D((X,)),
    ]
    vmem = pl.BlockSpec(memory_space=pltpu.VMEM)
    propagated, scores = pl.pallas_call(
        kernel,
        out_shape=(
            jax.ShapeDtypeStruct((channels, nodes), BF16),
            jax.ShapeDtypeStruct((1, queries), F32),
        ),
        in_specs=[vmem, pl.BlockSpec(memory_space=pl.ANY)] + [vmem] * 9,
        out_specs=(vmem, vmem),
        scratch_shapes=scratch,
        compiler_params=pltpu.CompilerParams(
            collective_id=0, has_side_effects=True, vmem_limit_bytes=56 * 1024 * 1024
        ),
    )(
        embed, tile_weight, tile_rows, tile_cols, send_rows,
        src_local.reshape(1, queries), dst_owner.reshape(1, queries), dst_local.reshape(1, queries),
        w_in, b_in.reshape(1, hidden), w_out.reshape(1, hidden),
    )
    return propagated, scores.reshape(queries)


def solution(mesh):
    placed = (
        P("feat", "node"),
        P("node", None, None, None),
        P("node", None),
        P("node", None),
        P("node", None),
        P("node"),
        P("node", None),
        P("node"),
        P("feat", None),
        P(),
        P(),
    )
    return jax.shard_map(
        shards,
        mesh=mesh,
        in_specs=placed,
        out_specs=(P("feat", "node"), P("node")),
        check_vma=False,
    )
```

```python
import jax
import jax.numpy as jnp
from jax import lax
from jax.experimental import pallas as pl
from jax.experimental.pallas import tpu as pltpu
from jax.sharding import PartitionSpec as P

Z, Y, C, X = 8, 8, 2, 4
RB, B, CAP = 8, 128, 8
HOPS = 2
TELEPORT = 0.1
MESH = pl.DeviceIdType.MESH
F32, BF16, I32 = jnp.float32, jnp.bfloat16, jnp.int32


def dot(left, right, left_dim, right_dim):
    return lax.dot_general(
        left, right, (((left_dim,), (right_dim,)), ((), ())), preferred_element_type=F32
    )


def iota(shape, dim):
    return lax.broadcasted_iota(I32, shape, dim)


def kernel(
    embed, weight_hbm, tile_rows, tile_cols, send_rows, src_local, dst_owner, dst_local, w_in, b_in, w_out,
    out, scores,
    cur0, cur1, cur2, gz0, gy0, gz1, gy1, sa0, sb0, sa1, sb1, ra0, rb0, ra1, rb1,
    weight, total, cols, table, table_s, sr_own, srz, sry, srz_s, sry_s,
    req, reqz, reqm, reqy, pick, pick_src, pick_slot, reply, mid, got,
    wfull, wt, bcol, ocol, had, hadfull,
    local_sem, sz_send, sz_recv, sy_send, sy_recv, a_send, a_recv, b_send, b_recv,
    qz_send, qz_recv, qy_send, qy_recv, pa_send, pa_recv, pb_send, pb_recv,
    rz_send, rz_recv, ry_send, ry_recv, wx_send, wx_recv, hx_send, hx_recv,
):
    parts = Z * Y * C
    yc, zc = Y * C, Z * C
    queries = src_local.shape[1]
    nodes = embed.shape[1]
    half = embed.shape[0] // 2
    me, xf = lax.axis_index("node"), lax.axis_index("feat")
    z, j = me // yc, me % yc
    y, c = j // C, j % C
    k = z * C + c

    def at_a(jd):
        return (z * yc + jd, xf)

    def at_b(kd):
        return (((kd // C) * Y + y) * C + kd % C, xf)

    def at_z(zd):
        return ((zd * Y + y) * C + c, xf)

    def at_y(yd):
        return ((z * Y + yd) * C + c, xf)

    def at_x(xd):
        return (me, xd)

    def push(src, dst, send, recv, device):
        return pltpu.make_async_remote_copy(
            src_ref=src, dst_ref=dst, send_sem=send, recv_sem=recv, device_id=device, device_id_type=MESH
        )

    def each(lo, hi, body):
        def step(i, carry):
            body(i)
            return carry
        lax.fori_loop(lo, hi, step, 0)

    def zigzag(i, n):
        return jnp.where(i % 2 == 1, (i + 1) // 2, n - i // 2)

    barrier = pltpu.get_barrier_semaphore()

    def greet(device):
        pl.semaphore_signal(barrier, inc=1, device_id=device, device_id_type=MESH)

    each(1, yc, lambda e: greet(at_a((j + e) % yc)))
    each(1, zc, lambda e: greet(at_b((k + e) % zc)))
    each(1, X, lambda e: greet(at_x((xf + e) % X)))

    fetch = pltpu.make_async_copy(weight_hbm.at[0], weight, local_sem.at[0])
    fetch.start()
    for r in range(RB):
        for h in range(2):
            cur0[h, r] = embed[h * half:(h + 1) * half, r * B:(r + 1) * B]
    sr_own[...] = send_rows[...].reshape(1, parts)

    pl.semaphore_wait(barrier, yc - 1 + zc - 1 + X - 1)

    def ring_copies(hop, gz, gy, step, piece, way):
        rows = pl.ds(piece * (RB // 2), RB // 2)
        sz, sy = (z - way * step) % Z, (y - way * step) % Y
        side = 0 if way == 1 else 1
        return (
            push(gz.at[sz, rows], gz.at[sz, rows], sz_send.at[hop, side, step, piece],
                 sz_recv.at[hop, side, step, piece], at_z((z + way) % Z)),
            push(gy.at[sy, rows], gy.at[sy, rows], sy_send.at[hop, side, step, piece],
                 sy_recv.at[hop, side, step, piece], at_y((y + way) % Y)),
        )

    ring = [
        (step, piece, way)
        for step in range(Z // 2) for piece in range(2) for way in (1, -1)
        if step < Z // 2 - 1 or piece == (0 if way == 1 else 1)
    ]

    def arrived(hop, gz, gy, step, piece, way):
        rows = pl.ds(piece * (RB // 2), RB // 2)
        sz, sy = (z - way * (step + 1)) % Z, (y - way * (step + 1)) % Y
        side = 0 if way == 1 else 1
        push(gz.at[sz, rows], gz.at[sz, rows], sz_send.at[hop, side, step, piece],
             sz_recv.at[hop, side, step, piece], at_z((z + way) % Z)).wait_recv()
        push(gy.at[sy, rows], gy.at[sy, rows], sy_send.at[hop, side, step, piece],
             sy_recv.at[hop, side, step, piece], at_y((y + way) % Y)).wait_recv()

    def share(hop, cur, gz, gy):
        gz[z] = cur[0]
        gy[y] = cur[1]
        for step, piece, way in ring:
            if step == 0:
                for copy in ring_copies(hop, gz, gy, step, piece, way):
                    copy.start()

    def shared(hop, gz, gy):
        passed = set()
        for step, piece, way in ring:
            if step > 0:
                arrived(hop, gz, gy, step - 1, piece, way)
                passed.add((step - 1, piece, way))
                for copy in ring_copies(hop, gz, gy, step, piece, way):
                    copy.start()
        for one in ring:
            if one not in passed:
                arrived(hop, gz, gy, *one)

    def deal(hop, gz, gy, sa, sb, ra, rb):
        def fill_a(jd, dst):
            for s in range(Z):
                dst[jd, s] = gz[s, srz_s[s, 0, z * yc + jd]]
        def fill_b(kd, dst):
            for s in range(Y):
                dst[kd, s] = gy[s, sry_s[s, 0, ((kd // C) * Y + y) * C + kd % C]]
        def go_a(jd):
            fill_a(jd, sa)
            push(sa.at[jd], ra.at[j], a_send.at[hop, jd], a_recv.at[hop, j], at_a(jd)).start()
        def go_b(kd):
            fill_b(kd, sb)
            push(sb.at[kd], rb.at[k], b_send.at[hop, kd], b_recv.at[hop, k], at_b(kd)).start()
        fill_a(j, ra)
        fill_b(k, rb)
        def ring_step(i):
            if C == 2:
                @pl.when(i == 0)
                def _():
                    go_a(y * C + 1 - c)
                    go_b(z * C + 1 - c)
            @pl.when(i > 0)
            def _():
                yd, zd = (y + zigzag(i, Y)) % Y, (z + zigzag(i, Z)) % Z
                for cd in range(C):
                    go_a(yd * C + cd)
                    go_b(zd * C + cd)
        each(0, Y, ring_step)

    def combine(hop, cur, sa, sb, ra, rb, nxt):
        def end_a(s):
            push(sa.at[s], ra.at[s], a_send.at[hop, s], a_recv.at[hop, s], at_a(s)).wait_recv()
        def end_b(s):
            push(sb.at[s], rb.at[s], b_send.at[hop, s], b_recv.at[hop, s], at_b(s)).wait_recv()
        def term(s, block):
            product = dot(block, weight[table_s[0, s]], 1, 1)
            total[s] = product + total[table_s[1, s]]
        def pair(s, zi, yi):
            zs, ys = (z + Z - zigzag(zi, Z)) % Z, (y + Y - zigzag(yi, Y)) % Y
            for cs in range(C):
                term(s * C + cs, jnp.concatenate([ra[ys * C + cs, zs], rb[zs * C + cs, ys]], axis=0))
        total[parts + RB] = jnp.zeros(total.shape[1:], F32)
        for n in range(Z):
            zs, ys = (z + Z - zigzag(n, Z)) % Z, (y + Y - zigzag(n, Y)) % Y
            if n > 0:
                for cs in range(C):
                    end_a(ys * C + cs)
                    end_b(zs * C + cs)
            elif C == 2:
                end_a(y * C + 1 - c)
                end_b(z * C + 1 - c)
            each(0, n + 1, lambda m: pair(n * n + m, n, m))
            if n > 0:
                each(0, n, lambda m: pair(n * n + n + 1 + m, m, n))
        for r in range(RB):
            term(parts + r, jnp.concatenate([cur[0, r], cur[1, r]], axis=0))
        for r in range(RB):
            first = jnp.concatenate([cur0[0, r], cur0[1, r]], axis=0).astype(F32)
            new = ((1.0 - TELEPORT) * total[parts + r] + TELEPORT * first).astype(BF16)
            nxt[0, r] = new[:half]
            nxt[1, r] = new[half:]

    share(0, cur0, gz0, gy0)

    def rows_z(d):
        push(sr_own, srz.at[z], rz_send.at[d], rz_recv.at[z], at_z((z + d) % Z)).start()
    def rows_y(d):
        push(sr_own, sry.at[y], ry_send.at[d], ry_recv.at[y], at_y((y + d) % Y)).start()
    each(1, Z, rows_z)
    each(1, Y, rows_y)
    srz[z] = sr_own[...]
    sry[y] = sr_own[...]
    each(1, X, lambda d: push(
        w_in, wfull.at[xf], wx_send.at[d], wx_recv.at[xf], at_x((xf + d) % X)).start())
    wfull[xf] = w_in[...]

    slots = cols.shape[1]
    cols[...] = jnp.full(cols.shape, -1, I32)
    tiles = tile_cols.shape[1]
    cols[0:1, 0:tiles] = tile_cols[...]
    cols[8:9, 0:tiles] = tile_rows[...]
    col = cols[0:1, :]
    peer = col - RB
    def ring_place(far, n):
        return jnp.where(far == 0, 0, jnp.where(far <= n // 2, 2 * far - 1, 2 * (n - far)))
    zi = ring_place((z + Z - peer // yc) % Z, Z)
    yi = ring_place((y + Y - peer % yc // C) % Y, Y)
    peer_slot = jnp.where(zi >= yi, zi * zi + yi, yi * yi + yi + 1 + zi) * C + peer % C
    slot_of = jnp.where(col < 0, -1, jnp.where(col < RB, parts + col, peer_slot))
    hit = (iota((slots, slots), 0) == slot_of).astype(F32).astype(BF16)
    kind = iota((8, slots), 0)
    facts = jnp.where(kind == 0, iota((8, slots), 1), jnp.where(kind == 1, cols[8:9, :], 1))
    found = dot(facts.astype(F32).astype(BF16), hit, 1, 1)
    row_of = jnp.where(found[2:3, :] > 0.5, found[1:2, :], -1.0)
    row_hit = (iota((128, slots), 0).astype(F32) == row_of).astype(F32).astype(BF16)
    same = dot(row_hit, row_hit, 0, 0)
    before = jnp.where(
        (same > 0.5) & (iota((slots, slots), 0) < iota((slots, slots), 1)), iota((slots, slots), 0).astype(F32), -1.0
    )
    last = jnp.max(before, axis=0, keepdims=True)
    table[0:1, :] = jnp.clip(found[0:1, :].astype(I32), 0, tiles - 1)
    table[1:2, :] = jnp.clip(jnp.where(last < 0.0, float(parts + RB), last).astype(I32), 0, parts + RB)
    to_smem = pltpu.make_async_copy(table, table_s, local_sem.at[1])
    to_smem.start()

    owner = dst_owner[...]
    owns = (iota((parts, queries), 0) == owner).astype(F32).astype(BF16)
    alike = dot(owns, owns, 0, 0)
    earlier = iota((queries, queries), 0) < iota((queries, queries), 1)
    rank = jnp.sum(jnp.where(earlier, alike, 0.0), axis=0, keepdims=True).astype(I32)
    place = iota((128, queries), 0) == rank
    high, low = dst_local[...] // 32, dst_local[...] % 32
    ask_high = dot(owns, jnp.where(place, high, 0).astype(F32).astype(BF16), 1, 1)
    ask_low = dot(owns, jnp.where(place, low, 0).astype(F32).astype(BF16), 1, 1)
    req[...] = (ask_high * 32.0 + ask_low).astype(I32).reshape(Z, yc, 128)
    def ask_z(d):
        zd = (z + d) % Z
        push(req.at[zd], reqz.at[z], qz_send.at[d], qz_recv.at[z], at_z(zd)).start()
    each(1, Z, ask_z)
    reqz[z] = req[z]
    fold = CAP // 2
    spot = owner * fold + rank % fold
    for side in range(2):
        spot_side = jnp.where(rank // fold == side, spot, -1)
        pick_slot[side] = (iota(pick_slot.shape[1:], 0) == spot_side).astype(F32).astype(BF16)
    pick_src[...] = (iota(pick_src.shape, 0) == src_local[...]).astype(F32).astype(BF16)

    def rows_z_end(d):
        s = (z + d) % Z
        push(sr_own, srz.at[s], rz_send.at[d], rz_recv.at[s], at_z(s)).wait_recv()
    def rows_y_end(d):
        s = (y + d) % Y
        push(sr_own, sry.at[s], ry_send.at[d], ry_recv.at[s], at_y(s)).wait_recv()
    each(1, Z, rows_z_end)
    each(1, Y, rows_y_end)
    rows_copies = [
        pltpu.make_async_copy(srz, srz_s, local_sem.at[2]),
        pltpu.make_async_copy(sry, sry_s, local_sem.at[3]),
    ]
    for copy in rows_copies:
        copy.start()
    for copy in rows_copies:
        copy.wait()
    shared(0, gz0, gy0)
    deal(0, gz0, gy0, sa0, sb0, ra0, rb0)

    def ask_z_end(d):
        s = (z + d) % Z
        push(req.at[s], reqz.at[s], qz_send.at[d], qz_recv.at[s], at_z(s)).wait_recv()
    each(1, Z, ask_z_end)
    for jd in range(yc):
        reqm[jd] = jnp.concatenate([reqz[s, jd:jd + 1, :] for s in range(Z)], axis=0)
    def ask_y(e):
        jd = (j + e) % yc
        push(reqm.at[jd], reqy.at[j], qy_send.at[e], qy_recv.at[j], at_a(jd)).start()
    each(1, yc, ask_y)
    reqy[j] = reqm[j]

    def w_end(d):
        s = (xf + d) % X
        push(w_in, wfull.at[s], wx_send.at[d], wx_recv.at[s], at_x(s)).wait_recv()
    each(1, X, w_end)
    hidden_units = w_in.shape[1]
    channels = w_in.shape[0]
    for n in range(hidden_units // 128):
        lanes = slice(n * 128, (n + 1) * 128)
        whole = jnp.concatenate([wfull[s, :, lanes] for s in range(X)], axis=0)
        wt[lanes, :] = whole.astype(F32).T.astype(BF16)
        bcol[lanes, :] = jnp.broadcast_to(b_in[0:1, lanes], (128, 128)).T
        ocol[lanes, :] = jnp.broadcast_to(w_out[0:1, lanes], (128, 128)).T

    to_smem.wait()
    fetch.wait()
    combine(0, cur0, sa0, sb0, ra0, rb0, cur1)

    share(1, cur1, gz1, gy1)
    shared(1, gz1, gy1)
    deal(1, gz1, gy1, sa1, sb1, ra1, rb1)

    def ask_y_end(e):
        s = (j + e) % yc
        push(reqm.at[s], reqy.at[s], qy_send.at[e], qy_recv.at[s], at_a(s)).wait_recv()
    each(1, yc, ask_y_end)
    asked = reqy[...].reshape(parts, 128).astype(F32)
    spread = (iota((parts * fold, parts), 0) // fold == iota((parts * fold, parts), 1)).astype(F32)
    wide = lax.dot_general(
        spread, asked, (((1,), (0,)), ((), ())), precision=lax.Precision.HIGHEST, preferred_element_type=F32
    )
    for side in range(2):
        mine = iota(wide.shape, 1) == iota(wide.shape, 0) % fold + side * fold
        node = jnp.sum(jnp.where(mine, wide, 0.0), axis=1, keepdims=True).astype(I32)
        pick[side] = (iota((parts * fold, nodes), 1) == node).astype(F32).astype(BF16)

    combine(1, cur1, sa1, sb1, ra1, rb1, cur2)
    for r in range(RB):
        for h in range(2):
            out[h * half:(h + 1) * half, r * B:(r + 1) * B] = cur2[h, r]

    final = out[...]
    rows = jnp.concatenate([dot(pick[side], final, 1, 1) for side in range(2)], axis=1)
    reply[...] = rows.reshape(yc, Z, fold, 2 * channels).astype(BF16)
    def reply_a(i):
        jd = (j + i) % yc
        push(reply.at[jd], mid.at[j], pa_send.at[i], pa_recv.at[j], at_a(jd)).start()
    each(1, yc, reply_a)
    mid[j] = reply[j]
    source = dot(final, pick_src[...], 1, 0)
    def reply_a_end(e):
        s = (j + e) % yc
        push(reply.at[s], mid.at[s], pa_send.at[e], pa_recv.at[s], at_a(s)).wait_recv()
    each(1, yc, reply_a_end)
    def reply_z(d):
        zd = (z + d) % Z
        push(mid.at[:, zd], got.at[z], pb_send.at[d], pb_recv.at[z], at_z(zd)).start()
    each(1, Z, reply_z)
    got[z] = mid[:, z]
    def reply_z_end(d):
        s = (z + d) % Z
        push(mid.at[:, s], got.at[s], pb_send.at[d], pb_recv.at[s], at_z(s)).wait_recv()
    each(1, Z, reply_z_end)
    replies = got[...].reshape(parts * fold, 2 * channels)
    target = dot(replies, pick_slot[0], 0, 0)[:channels] + dot(replies, pick_slot[1], 0, 0)[channels:]
    had[...] = (source * target).astype(BF16)
    def had_x(d):
        push(had, hadfull.at[xf], hx_send.at[d], hx_recv.at[xf], at_x((xf + d) % X)).start()
    each(1, X, had_x)
    hadfull[xf] = had[...]
    def had_x_end(d):
        s = (xf + d) % X
        push(had, hadfull.at[s], hx_send.at[d], hx_recv.at[s], at_x(s)).wait_recv()
    each(1, X, had_x_end)
    everything = hadfull[...].reshape(X * channels, queries)
    score = jnp.zeros((8, queries), F32)
    for n in range(hidden_units // 128):
        lanes = slice(n * 128, (n + 1) * 128)
        hidden = dot(wt[lanes, :], everything, 1, 0)
        bias, gain = bcol[lanes, :], ocol[lanes, :]
        if queries > 128:
            bias, gain = (jnp.concatenate([v] * (queries // 128), axis=1) for v in (bias, gain))
        else:
            bias, gain = bias[:, :queries], gain[:, :queries]
        active = jnp.maximum(hidden + bias, 0.0) * gain
        score = score + jnp.sum(active.reshape(16, 8, queries), axis=0)
    scores[...] = jnp.sum(score, axis=0, keepdims=True)

    for hop, gz, gy, sa, sb, ra, rb in (
        (0, gz0, gy0, sa0, sb0, ra0, rb0), (1, gz1, gy1, sa1, sb1, ra1, rb1)
    ):
        for one in ring:
            for copy in ring_copies(hop, gz, gy, *one):
                copy.wait_send()
        def left_a(e):
            jd = (j + e) % yc
            push(sa.at[jd], ra.at[j], a_send.at[hop, jd], a_recv.at[hop, j], at_a(jd)).wait_send()
        def left_b(e):
            kd = (k + e) % zc
            push(sb.at[kd], rb.at[k], b_send.at[hop, kd], b_recv.at[hop, k], at_b(kd)).wait_send()
        each(1, yc, left_a)
        each(1, zc, left_b)
    def left_z(d):
        zd = (z + d) % Z
        push(sr_own, srz.at[z], rz_send.at[d], rz_recv.at[z], at_z(zd)).wait_send()
        push(req.at[zd], reqz.at[z], qz_send.at[d], qz_recv.at[z], at_z(zd)).wait_send()
        push(mid.at[:, zd], got.at[z], pb_send.at[d], pb_recv.at[z], at_z(zd)).wait_send()
    each(1, Z, left_z)
    each(1, Y, lambda d: push(
        sr_own, sry.at[y], ry_send.at[d], ry_recv.at[y], at_y((y + d) % Y)).wait_send())
    def left_y(e):
        jd = (j + e) % yc
        push(reqm.at[jd], reqy.at[j], qy_send.at[e], qy_recv.at[j], at_a(jd)).wait_send()
        push(reply.at[jd], mid.at[j], pa_send.at[e], pa_recv.at[j], at_a(jd)).wait_send()
    each(1, yc, left_y)
    def left_x(d):
        xd = (xf + d) % X
        push(w_in, wfull.at[xf], wx_send.at[d], wx_recv.at[xf], at_x(xd)).wait_send()
        push(had, hadfull.at[xf], hx_send.at[d], hx_recv.at[xf], at_x(xd)).wait_send()
    each(1, X, left_x)


def shards(
    embed, tile_weight, tile_rows, tile_cols, send_rows, src_local, dst_owner, dst_local, w_in, b_in, w_out
):
    parts, yc, zc = Z * Y * C, Y * C, Z * C
    channels, nodes = embed.shape
    half = channels // 2
    queries, hidden = src_local.shape[0], w_in.shape[1]
    tiles = tile_rows.shape[1]
    slots, fold = 256, CAP // 2
    V, S, D = pltpu.VMEM, pltpu.SMEM, pltpu.SemaphoreType.DMA
    cur = [V((2, RB, half, B), BF16)] * 3
    near = [V((n, RB, half, B), BF16) for n in (Z, Y, Z, Y)]
    deal = [V((n, m, half, B), BF16) for n, m in ((yc, Z), (zc, Y))]
    scratch = cur + near + deal * 4 + [
        V((tiles, B, B), BF16), V((parts + RB + 1, channels, B), F32),
        V((16, slots), I32), V((8, slots), I32), S((8, slots), I32),
        V((1, parts), I32), V((Z, 1, parts), I32), V((Y, 1, parts), I32), S((Z, 1, parts), I32), S((Y, 1, parts), I32),
        V((Z, yc, 128), I32), V((Z, yc, 128), I32), V((yc, Z, 128), I32), V((yc, Z, 128), I32),
        V((2, parts * fold, nodes), BF16), V((nodes, queries), BF16), V((2, parts * fold, queries), BF16),
        V((yc, Z, fold, 2 * channels), BF16), V((yc, Z, fold, 2 * channels), BF16), V((Z, yc, fold, 2 * channels), BF16),
        V((X, channels, hidden), BF16), V((hidden, X * channels), BF16), V((hidden, 128), F32), V((hidden, 128), F32),
        V((channels, queries), BF16), V((X, channels, queries), BF16),
        D((4,)), D((HOPS, 2, Z // 2, 2)), D((HOPS, 2, Z // 2, 2)), D((HOPS, 2, Y // 2, 2)), D((HOPS, 2, Y // 2, 2)),
        D((HOPS, yc)), D((HOPS, yc)), D((HOPS, zc)), D((HOPS, zc)),
        D((Z,)), D((Z,)), D((yc,)), D((yc,)), D((yc,)), D((yc,)), D((Z,)), D((Z,)),
        D((Z,)), D((Z,)), D((Y,)), D((Y,)), D((X,)), D((X,)), D((X,)), D((X,)),
    ]
    vmem = pl.BlockSpec(memory_space=pltpu.VMEM)
    propagated, scores = pl.pallas_call(
        kernel,
        out_shape=(
            jax.ShapeDtypeStruct((channels, nodes), BF16),
            jax.ShapeDtypeStruct((1, queries), F32),
        ),
        in_specs=[vmem, pl.BlockSpec(memory_space=pl.ANY)] + [vmem] * 9,
        out_specs=(vmem, vmem),
        scratch_shapes=scratch,
        compiler_params=pltpu.CompilerParams(
            collective_id=0, has_side_effects=True, vmem_limit_bytes=56 * 1024 * 1024
        ),
    )(
        embed, tile_weight, tile_rows, tile_cols, send_rows,
        src_local.reshape(1, queries), dst_owner.reshape(1, queries), dst_local.reshape(1, queries),
        w_in, b_in.reshape(1, hidden), w_out.reshape(1, hidden),
    )
    return propagated, scores.reshape(queries)


def solution(mesh):
    placed = (
        P("feat", "node"),
        P("node", None, None, None),
        P("node", None),
        P("node", None),
        P("node", None),
        P("node"),
        P("node", None),
        P("node"),
        P("feat", None),
        P(),
        P(),
    )
    return jax.shard_map(
        shards,
        mesh=mesh,
        in_specs=placed,
        out_specs=(P("feat", "node"), P("node")),
        check_vma=False,
    )
```

```python
import jax
import jax.numpy as jnp
from jax import lax
from jax.experimental import pallas as pl
from jax.experimental.pallas import tpu as pltpu
from jax.sharding import PartitionSpec as P

Z, Y, C, X = 8, 8, 2, 4
RB, B, CAP = 8, 128, 8
HOPS = 2
TELEPORT = 0.1
MESH = pl.DeviceIdType.MESH
F32, BF16, I32 = jnp.float32, jnp.bfloat16, jnp.int32


def dot(left, right, left_dim, right_dim):
    return lax.dot_general(
        left, right, (((left_dim,), (right_dim,)), ((), ())), preferred_element_type=F32
    )


def iota(shape, dim):
    return lax.broadcasted_iota(I32, shape, dim)


def kernel(
    embed_in, weight_hbm, tile_rows_in, tile_cols_in, send_rows_in, src_local_in, dst_owner_in, dst_local_in,
    w_in_in, b_in_in, w_out_in, out, scores,
    embed, tile_rows, tile_cols, sr_own, src_local, dst_owner, dst_local, w_in, b_in, w_out,
    cur0, cur1, cur2, gz0, gy0, gz1, gy1, sa0, sb0, sa1, sb1, ra0, rb0, ra1, rb1,
    weight, total, own, cols, table, table_s, srz, sry, srz_s, sry_s,
    req, reqz, reqm, reqy, pick, pick_src, pick_slot, reply, mid, got,
    wfull, wt, bcol, ocol, had, hadfull,
    local_sem, sz_send, sz_recv, sy_send, sy_recv, a_send, a_recv, b_send, b_recv,
    qz_send, qz_recv, qy_send, qy_recv, pa_send, pa_recv, pb_send, pb_recv,
    rz_send, rz_recv, ry_send, ry_recv, wx_send, wx_recv, hx_send, hx_recv,
):
    parts = Z * Y * C
    yc, zc = Y * C, Z * C
    queries = src_local.shape[1]
    nodes = embed.shape[1]
    half = embed.shape[0] // 2
    me, xf = lax.axis_index("node"), lax.axis_index("feat")
    z, j = me // yc, me % yc
    y, c = j // C, j % C
    k = z * C + c

    def at_a(jd):
        return (z * yc + jd, xf)

    def at_b(kd):
        return (((kd // C) * Y + y) * C + kd % C, xf)

    def at_z(zd):
        return ((zd * Y + y) * C + c, xf)

    def at_y(yd):
        return ((z * Y + yd) * C + c, xf)

    def at_x(xd):
        return (me, xd)

    def push(src, dst, send, recv, device):
        return pltpu.make_async_remote_copy(
            src_ref=src, dst_ref=dst, send_sem=send, recv_sem=recv, device_id=device, device_id_type=MESH
        )

    def each(lo, hi, body):
        def step(i, carry):
            body(i)
            return carry
        lax.fori_loop(lo, hi, step, 0)

    def zigzag(i, n):
        return jnp.where(i % 2 == 1, (i + 1) // 2, n - i // 2)

    barrier = pltpu.get_barrier_semaphore()

    def greet(device):
        pl.semaphore_signal(barrier, inc=1, device_id=device, device_id_type=MESH)

    ins = [
        pltpu.make_async_copy(src, dst, local_sem.at[4 + n]) for n, (src, dst) in enumerate((
            (embed_in, embed), (send_rows_in, sr_own), (w_in_in, w_in), (tile_rows_in, tile_rows),
            (tile_cols_in, tile_cols), (src_local_in, src_local), (dst_owner_in, dst_owner),
            (dst_local_in, dst_local), (b_in_in, b_in), (w_out_in, w_out),
        ))
    ]
    ins[0].start()
    ins[1].start()
    each(1, yc, lambda e: greet(at_a((j + e) % yc)))
    each(1, zc, lambda e: greet(at_b((k + e) % zc)))
    each(1, X, lambda e: greet(at_x((xf + e) % X)))

    fetch = pltpu.make_async_copy(weight_hbm.at[0], weight, local_sem.at[0])
    for copy in ins[2:]:
        copy.start()
    fetch.start()
    ins[0].wait()
    ins[1].wait()
    for r in range(RB):
        for h in range(2):
            cur0[h, r] = embed[h * half:(h + 1) * half, r * B:(r + 1) * B]

    pl.semaphore_wait(barrier, yc - 1 + zc - 1 + X - 1)

    def ring_copies(hop, gz, gy, step, piece, way):
        rows = pl.ds(piece * (RB // 2), RB // 2)
        sz, sy = (z - way * step) % Z, (y - way * step) % Y
        side = 0 if way == 1 else 1
        return (
            push(gz.at[sz, rows], gz.at[sz, rows], sz_send.at[hop, side, step, piece],
                 sz_recv.at[hop, side, step, piece], at_z((z + way) % Z)),
            push(gy.at[sy, rows], gy.at[sy, rows], sy_send.at[hop, side, step, piece],
                 sy_recv.at[hop, side, step, piece], at_y((y + way) % Y)),
        )

    ring = [
        (step, piece, way)
        for step in range(Z // 2) for piece in range(2) for way in (1, -1)
        if step < Z // 2 - 1 or piece == (0 if way == 1 else 1)
    ]

    def arrived(hop, gz, gy, step, piece, way):
        rows = pl.ds(piece * (RB // 2), RB // 2)
        sz, sy = (z - way * (step + 1)) % Z, (y - way * (step + 1)) % Y
        side = 0 if way == 1 else 1
        push(gz.at[sz, rows], gz.at[sz, rows], sz_send.at[hop, side, step, piece],
             sz_recv.at[hop, side, step, piece], at_z((z + way) % Z)).wait_recv()
        push(gy.at[sy, rows], gy.at[sy, rows], sy_send.at[hop, side, step, piece],
             sy_recv.at[hop, side, step, piece], at_y((y + way) % Y)).wait_recv()

    def share(hop, cur, gz, gy):
        gz[z] = cur[0]
        gy[y] = cur[1]
        for step, piece, way in ring:
            if step == 0:
                for copy in ring_copies(hop, gz, gy, step, piece, way):
                    copy.start()

    def shared(hop, gz, gy):
        passed = set()
        for step, piece, way in ring:
            if step > 0:
                arrived(hop, gz, gy, step - 1, piece, way)
                passed.add((step - 1, piece, way))
                for copy in ring_copies(hop, gz, gy, step, piece, way):
                    copy.start()
        for one in ring:
            if one not in passed:
                arrived(hop, gz, gy, *one)

    def deal(hop, gz, gy, sa, sb, ra, rb):
        def fill_a(jd, dst):
            for s in range(Z):
                dst[jd, s] = gz[s, srz_s[s, 0, z * yc + jd]]
        def fill_b(kd, dst):
            for s in range(Y):
                dst[kd, s] = gy[s, sry_s[s, 0, ((kd // C) * Y + y) * C + kd % C]]
        def go_a(jd):
            fill_a(jd, sa)
            push(sa.at[jd], ra.at[j], a_send.at[hop, jd], a_recv.at[hop, j], at_a(jd)).start()
        def go_b(kd):
            fill_b(kd, sb)
            push(sb.at[kd], rb.at[k], b_send.at[hop, kd], b_recv.at[hop, k], at_b(kd)).start()
        fill_a(j, ra)
        fill_b(k, rb)
        def ring_step(i):
            if C == 2:
                @pl.when(i == 0)
                def _():
                    go_a(y * C + 1 - c)
                    go_b(z * C + 1 - c)
            @pl.when(i > 0)
            def _():
                yd, zd = (y + zigzag(i, Y)) % Y, (z + zigzag(i, Z)) % Z
                for cd in range(C):
                    go_a(yd * C + cd)
                    go_b(zd * C + cd)
        each(0, Y, ring_step)

    def combine(hop, cur, sa, sb, ra, rb, nxt):
        def end_a(s):
            push(sa.at[s], ra.at[s], a_send.at[hop, s], a_recv.at[hop, s], at_a(s)).wait_recv()
        def end_b(s):
            push(sb.at[s], rb.at[s], b_send.at[hop, s], b_recv.at[hop, s], at_b(s)).wait_recv()
        def term(s, block):
            product = dot(block, weight[table_s[0, s]], 1, 1)
            total[s] = product + total[table_s[1, s]]
        def pair(s, zi, yi):
            zs, ys = (z + Z - zigzag(zi, Z)) % Z, (y + Y - zigzag(yi, Y)) % Y
            for cs in range(C):
                term(s * C + cs, jnp.concatenate([ra[ys * C + cs, zs], rb[zs * C + cs, ys]], axis=0))
        def corner(n, m):
            pair(n * n + 2 * m, n, m)
            pair(n * n + 2 * m + 1, m, n)
        total[parts] = jnp.zeros(total.shape[1:], F32)
        for r in range(RB):
            block = jnp.concatenate([cur[0, r], cur[1, r]], axis=0)
            own[r] = dot(block, weight[table_s[0, parts + r]], 1, 1)
        for n in range(Z):
            zs, ys = (z + Z - zigzag(n, Z)) % Z, (y + Y - zigzag(n, Y)) % Y
            if n > 0:
                for cs in range(C):
                    end_a(ys * C + cs)
                    end_b(zs * C + cs)
            elif C == 2:
                end_a(y * C + 1 - c)
                end_b(z * C + 1 - c)
            def corners(m):
                corner(n, 2 * m)
                corner(n, 2 * m + 1)
            each(0, n // 2, corners)
            if n % 2 == 1:
                corner(n, n - 1)
            pair(n * n + 2 * n, n, n)
        for r in range(RB):
            first = jnp.concatenate([cur0[0, r], cur0[1, r]], axis=0).astype(F32)
            summed = total[table_s[1, parts + r]] + own[r]
            new = ((1.0 - TELEPORT) * summed + TELEPORT * first).astype(BF16)
            nxt[0, r] = new[:half]
            nxt[1, r] = new[half:]

    share(0, cur0, gz0, gy0)

    def rows_z(d):
        push(sr_own, srz.at[z], rz_send.at[d], rz_recv.at[z], at_z((z + d) % Z)).start()
    def rows_y(d):
        push(sr_own, sry.at[y], ry_send.at[d], ry_recv.at[y], at_y((y + d) % Y)).start()
    each(1, Z, rows_z)
    each(1, Y, rows_y)
    srz[z] = sr_own[...]
    sry[y] = sr_own[...]
    ins[2].wait()
    each(1, X, lambda d: push(
        w_in, wfull.at[xf], wx_send.at[d], wx_recv.at[xf], at_x((xf + d) % X)).start())
    wfull[xf] = w_in[...]

    def rows_z_end(d):
        s = (z + d) % Z
        push(sr_own, srz.at[s], rz_send.at[d], rz_recv.at[s], at_z(s)).wait_recv()
    def rows_y_end(d):
        s = (y + d) % Y
        push(sr_own, sry.at[s], ry_send.at[d], ry_recv.at[s], at_y(s)).wait_recv()
    each(1, Z, rows_z_end)
    each(1, Y, rows_y_end)
    rows_copies = [
        pltpu.make_async_copy(srz, srz_s, local_sem.at[2]),
        pltpu.make_async_copy(sry, sry_s, local_sem.at[3]),
    ]
    for copy in rows_copies:
        copy.start()
    for copy in rows_copies:
        copy.wait()
    shared(0, gz0, gy0)
    deal(0, gz0, gy0, sa0, sb0, ra0, rb0)

    for copy in ins[3:]:
        copy.wait()
    slots = cols.shape[1]
    cols[...] = jnp.full(cols.shape, -1, I32)
    tiles = tile_cols.shape[1]
    cols[0:1, 0:tiles] = tile_cols[...]
    cols[8:9, 0:tiles] = tile_rows[...]
    col = cols[0:1, :]
    peer = col - RB
    def ring_place(far, n):
        return jnp.where(far == 0, 0, jnp.where(far <= n // 2, 2 * far - 1, 2 * (n - far)))
    zi = ring_place((z + Z - peer // yc) % Z, Z)
    yi = ring_place((y + Y - peer % yc // C) % Y, Y)
    peer_slot = (jnp.maximum(zi, yi) * jnp.maximum(zi, yi) + 2 * jnp.minimum(zi, yi) + jnp.where(yi > zi, 1, 0)) * C + peer % C
    slot_of = jnp.where(col < 0, -1, jnp.where(col < RB, parts + col, peer_slot))
    hit = (iota((slots, slots), 0) == slot_of).astype(F32).astype(BF16)
    kind = iota((8, slots), 0)
    facts = jnp.where(kind == 0, iota((8, slots), 1), jnp.where(kind == 1, cols[8:9, :], 1))
    found = dot(facts.astype(F32).astype(BF16), hit, 1, 1)
    row_of = jnp.where(found[2:3, :] > 0.5, found[1:2, :], -1.0)
    row_hit = (iota((128, slots), 0).astype(F32) == row_of).astype(F32).astype(BF16)
    same = dot(row_hit, row_hit, 0, 0)
    before = jnp.where(
        (same > 0.5) & (iota((slots, slots), 0) < iota((slots, slots), 1)), iota((slots, slots), 0).astype(F32), -1.0
    )
    last = jnp.max(before, axis=0, keepdims=True)
    table[0:1, :] = jnp.clip(found[0:1, :].astype(I32), 0, tiles - 1)
    table[1:2, :] = jnp.clip(jnp.where(last < 0.0, float(parts), last).astype(I32), 0, parts)
    to_smem = pltpu.make_async_copy(table, table_s, local_sem.at[1])
    to_smem.start()

    owner = dst_owner[...]
    owns = (iota((parts, queries), 0) == owner).astype(F32).astype(BF16)
    alike = dot(owns, owns, 0, 0)
    earlier = iota((queries, queries), 0) < iota((queries, queries), 1)
    rank = jnp.sum(jnp.where(earlier, alike, 0.0), axis=0, keepdims=True).astype(I32)
    place = iota((128, queries), 0) == rank
    high, low = dst_local[...] // 32, dst_local[...] % 32
    ask_high = dot(owns, jnp.where(place, high, 0).astype(F32).astype(BF16), 1, 1)
    ask_low = dot(owns, jnp.where(place, low, 0).astype(F32).astype(BF16), 1, 1)
    req[...] = (ask_high * 32.0 + ask_low).astype(I32).reshape(Z, yc, 128)
    def ask_z(d):
        zd = (z + d) % Z
        push(req.at[zd], reqz.at[z], qz_send.at[d], qz_recv.at[z], at_z(zd)).start()
    each(1, Z, ask_z)
    reqz[z] = req[z]
    fold = CAP // 2
    spot = owner * fold + rank % fold
    for side in range(2):
        spot_side = jnp.where(rank // fold == side, spot, -1)
        pick_slot[side] = (iota(pick_slot.shape[1:], 0) == spot_side).astype(F32).astype(BF16)
    pick_src[...] = (iota(pick_src.shape, 0) == src_local[...]).astype(F32).astype(BF16)

    def w_end(d):
        s = (xf + d) % X
        push(w_in, wfull.at[s], wx_send.at[d], wx_recv.at[s], at_x(s)).wait_recv()
    each(1, X, w_end)
    hidden_units = w_in.shape[1]
    channels = w_in.shape[0]
    for n in range(hidden_units // 128):
        lanes = slice(n * 128, (n + 1) * 128)
        whole = jnp.concatenate([wfull[s, :, lanes] for s in range(X)], axis=0)
        wt[lanes, :] = whole.astype(F32).T.astype(BF16)
        bcol[lanes, :] = jnp.broadcast_to(b_in[0:1, lanes], (128, 128)).T
        ocol[lanes, :] = jnp.broadcast_to(w_out[0:1, lanes], (128, 128)).T

    to_smem.wait()
    fetch.wait()
    combine(0, cur0, sa0, sb0, ra0, rb0, cur1)

    share(1, cur1, gz1, gy1)

    def ask_z_end(d):
        s = (z + d) % Z
        push(req.at[s], reqz.at[s], qz_send.at[d], qz_recv.at[s], at_z(s)).wait_recv()
    each(1, Z, ask_z_end)
    for jd in range(yc):
        reqm[jd] = jnp.concatenate([reqz[s, jd:jd + 1, :] for s in range(Z)], axis=0)
    def ask_y(e):
        jd = (j + e) % yc
        push(reqm.at[jd], reqy.at[j], qy_send.at[e], qy_recv.at[j], at_a(jd)).start()
    each(1, yc, ask_y)
    reqy[j] = reqm[j]

    shared(1, gz1, gy1)
    deal(1, gz1, gy1, sa1, sb1, ra1, rb1)

    def ask_y_end(e):
        s = (j + e) % yc
        push(reqm.at[s], reqy.at[s], qy_send.at[e], qy_recv.at[s], at_a(s)).wait_recv()
    each(1, yc, ask_y_end)
    asked = reqy[...].reshape(parts, 128).astype(F32)
    spread = (iota((parts * fold, parts), 0) // fold == iota((parts * fold, parts), 1)).astype(F32)
    wide = lax.dot_general(
        spread, asked, (((1,), (0,)), ((), ())), precision=lax.Precision.HIGHEST, preferred_element_type=F32
    )
    for side in range(2):
        mine = iota(wide.shape, 1) == iota(wide.shape, 0) % fold + side * fold
        node = jnp.sum(jnp.where(mine, wide, 0.0), axis=1, keepdims=True).astype(I32)
        pick[side] = (iota((parts * fold, nodes), 1) == node).astype(F32).astype(BF16)

    combine(1, cur1, sa1, sb1, ra1, rb1, cur2)
    for r in range(RB):
        for h in range(2):
            out[h * half:(h + 1) * half, r * B:(r + 1) * B] = cur2[h, r]

    final = out[...]
    rows = jnp.concatenate([dot(pick[side], final, 1, 1) for side in range(2)], axis=1)
    reply[...] = rows.reshape(yc, Z, fold, 2 * channels).astype(BF16)
    def reply_a(i):
        jd = (j + i) % yc
        push(reply.at[jd], mid.at[j], pa_send.at[i], pa_recv.at[j], at_a(jd)).start()
    each(1, yc, reply_a)
    mid[j] = reply[j]
    source = dot(final, pick_src[...], 1, 0)
    def reply_a_end(e):
        s = (j + e) % yc
        push(reply.at[s], mid.at[s], pa_send.at[e], pa_recv.at[s], at_a(s)).wait_recv()
    each(1, yc, reply_a_end)
    def reply_z(d):
        zd = (z + d) % Z
        push(mid.at[:, zd], got.at[z], pb_send.at[d], pb_recv.at[z], at_z(zd)).start()
    each(1, Z, reply_z)
    got[z] = mid[:, z]
    def reply_z_end(d):
        s = (z + d) % Z
        push(mid.at[:, s], got.at[s], pb_send.at[d], pb_recv.at[s], at_z(s)).wait_recv()
    each(1, Z, reply_z_end)
    replies = got[...].reshape(parts * fold, 2 * channels)
    target = dot(replies, pick_slot[0], 0, 0)[:channels] + dot(replies, pick_slot[1], 0, 0)[channels:]
    had[...] = (source * target).astype(BF16)
    def had_x(d):
        push(had, hadfull.at[xf], hx_send.at[d], hx_recv.at[xf], at_x((xf + d) % X)).start()
    each(1, X, had_x)
    hadfull[xf] = had[...]
    def had_x_end(d):
        s = (xf + d) % X
        push(had, hadfull.at[s], hx_send.at[d], hx_recv.at[s], at_x(s)).wait_recv()
    each(1, X, had_x_end)
    everything = hadfull[...].reshape(X * channels, queries)
    score = jnp.zeros((8, queries), F32)
    for n in range(hidden_units // 128):
        lanes = slice(n * 128, (n + 1) * 128)
        hidden = dot(wt[lanes, :], everything, 1, 0)
        bias, gain = bcol[lanes, :], ocol[lanes, :]
        if queries > 128:
            bias, gain = (jnp.concatenate([v] * (queries // 128), axis=1) for v in (bias, gain))
        else:
            bias, gain = bias[:, :queries], gain[:, :queries]
        active = jnp.maximum(hidden + bias, 0.0) * gain
        score = score + jnp.sum(active.reshape(16, 8, queries), axis=0)
    scores[...] = jnp.sum(score, axis=0, keepdims=True)

    for hop, gz, gy, sa, sb, ra, rb in (
        (0, gz0, gy0, sa0, sb0, ra0, rb0), (1, gz1, gy1, sa1, sb1, ra1, rb1)
    ):
        for one in ring:
            for copy in ring_copies(hop, gz, gy, *one):
                copy.wait_send()
        def left_a(e):
            jd = (j + e) % yc
            push(sa.at[jd], ra.at[j], a_send.at[hop, jd], a_recv.at[hop, j], at_a(jd)).wait_send()
        def left_b(e):
            kd = (k + e) % zc
            push(sb.at[kd], rb.at[k], b_send.at[hop, kd], b_recv.at[hop, k], at_b(kd)).wait_send()
        each(1, yc, left_a)
        each(1, zc, left_b)
    def left_z(d):
        zd = (z + d) % Z
        push(sr_own, srz.at[z], rz_send.at[d], rz_recv.at[z], at_z(zd)).wait_send()
        push(req.at[zd], reqz.at[z], qz_send.at[d], qz_recv.at[z], at_z(zd)).wait_send()
        push(mid.at[:, zd], got.at[z], pb_send.at[d], pb_recv.at[z], at_z(zd)).wait_send()
    each(1, Z, left_z)
    each(1, Y, lambda d: push(
        sr_own, sry.at[y], ry_send.at[d], ry_recv.at[y], at_y((y + d) % Y)).wait_send())
    def left_y(e):
        jd = (j + e) % yc
        push(reqm.at[jd], reqy.at[j], qy_send.at[e], qy_recv.at[j], at_a(jd)).wait_send()
        push(reply.at[jd], mid.at[j], pa_send.at[e], pa_recv.at[j], at_a(jd)).wait_send()
    each(1, yc, left_y)
    def left_x(d):
        xd = (xf + d) % X
        push(w_in, wfull.at[xf], wx_send.at[d], wx_recv.at[xf], at_x(xd)).wait_send()
        push(had, hadfull.at[xf], hx_send.at[d], hx_recv.at[xf], at_x(xd)).wait_send()
    each(1, X, left_x)


def shards(
    embed, tile_weight, tile_rows, tile_cols, send_rows, src_local, dst_owner, dst_local, w_in, b_in, w_out
):
    parts, yc, zc = Z * Y * C, Y * C, Z * C
    channels, nodes = embed.shape
    half = channels // 2
    queries, hidden = src_local.shape[0], w_in.shape[1]
    tiles = tile_rows.shape[1]
    slots, fold = 256, CAP // 2
    V, S, D = pltpu.VMEM, pltpu.SMEM, pltpu.SemaphoreType.DMA
    cur = [V((2, RB, half, B), BF16)] * 3
    near = [V((n, RB, half, B), BF16) for n in (Z, Y, Z, Y)]
    deal = [V((n, m, half, B), BF16) for n, m in ((yc, Z), (zc, Y))]
    staged = [
        V((channels, nodes), BF16), V((1, tiles), I32), V((1, tiles), I32), V((1, parts), I32),
        V((1, queries), I32), V((1, queries), I32), V((1, queries), I32),
        V((channels, hidden), BF16), V((1, hidden), F32), V((1, hidden), F32),
    ]
    scratch = staged + cur + near + deal * 4 + [
        V((tiles, B, B), BF16), V((parts + 1, channels, B), F32), V((RB, channels, B), F32),
        V((16, slots), I32), V((8, slots), I32), S((8, slots), I32),
        V((Z, 1, parts), I32), V((Y, 1, parts), I32), S((Z, 1, parts), I32), S((Y, 1, parts), I32),
        V((Z, yc, 128), I32), V((Z, yc, 128), I32), V((yc, Z, 128), I32), V((yc, Z, 128), I32),
        V((2, parts * fold, nodes), BF16), V((nodes, queries), BF16), V((2, parts * fold, queries), BF16),
        V((yc, Z, fold, 2 * channels), BF16), V((yc, Z, fold, 2 * channels), BF16), V((Z, yc, fold, 2 * channels), BF16),
        V((X, channels, hidden), BF16), V((hidden, X * channels), BF16), V((hidden, 128), F32), V((hidden, 128), F32),
        V((channels, queries), BF16), V((X, channels, queries), BF16),
        D((14,)), D((HOPS, 2, Z // 2, 2)), D((HOPS, 2, Z // 2, 2)), D((HOPS, 2, Y // 2, 2)), D((HOPS, 2, Y // 2, 2)),
        D((HOPS, yc)), D((HOPS, yc)), D((HOPS, zc)), D((HOPS, zc)),
        D((Z,)), D((Z,)), D((yc,)), D((yc,)), D((yc,)), D((yc,)), D((Z,)), D((Z,)),
        D((Z,)), D((Z,)), D((Y,)), D((Y,)), D((X,)), D((X,)), D((X,)), D((X,)),
    ]
    vmem = pl.BlockSpec(memory_space=pltpu.VMEM)
    propagated, scores = pl.pallas_call(
        kernel,
        out_shape=(
            jax.ShapeDtypeStruct((channels, nodes), BF16),
            jax.ShapeDtypeStruct((1, queries), F32),
        ),
        in_specs=[pl.BlockSpec(memory_space=pl.ANY)] * 11,
        out_specs=(vmem, vmem),
        scratch_shapes=scratch,
        compiler_params=pltpu.CompilerParams(
            collective_id=0, has_side_effects=True, vmem_limit_bytes=56 * 1024 * 1024
        ),
    )(
        embed, tile_weight, tile_rows, tile_cols, send_rows,
        src_local.reshape(1, queries), dst_owner.reshape(1, queries), dst_local.reshape(1, queries),
        w_in, b_in.reshape(1, hidden), w_out.reshape(1, hidden),
    )
    return propagated, scores.reshape(queries)


def solution(mesh):
    placed = (
        P("feat", "node"),
        P("node", None, None, None),
        P("node", None),
        P("node", None),
        P("node", None),
        P("node"),
        P("node", None),
        P("node"),
        P("feat", None),
        P(),
        P(),
    )
    return jax.shard_map(
        shards,
        mesh=mesh,
        in_specs=placed,
        out_specs=(P("feat", "node"), P("node")),
        check_vma=False,
    )
```

```python
import jax
import jax.numpy as jnp
from jax import lax
from jax.experimental import pallas as pl
from jax.experimental.pallas import tpu as pltpu
from jax.sharding import PartitionSpec as P

Z, Y, C, X = 8, 8, 2, 4
RB, B, CAP = 8, 128, 8
HOPS = 2
TELEPORT = 0.1
MESH = pl.DeviceIdType.MESH
F32, BF16, I32 = jnp.float32, jnp.bfloat16, jnp.int32


def dot(left, right, left_dim, right_dim):
    return lax.dot_general(
        left, right, (((left_dim,), (right_dim,)), ((), ())), preferred_element_type=F32
    )


def iota(shape, dim):
    return lax.broadcasted_iota(I32, shape, dim)


def kernel(
    embed_in, weight_hbm, tile_rows_in, tile_cols_in, send_rows_in, src_local_in, dst_owner_in, dst_local_in,
    w_in_in, b_in_in, w_out_in, out, scores,
    embed, tile_rows, tile_cols, sr_own, src_local, dst_owner, dst_local, w_in, b_in, w_out,
    cur0, cur1, cur2, gz0, gy0, gz1, gy1, fz0, fy0, fz1, fy1, sa0, sb0, sa1, sb1, ra0, rb0, ra1, rb1,
    weight, total, own, cols, table, table_s, srz, sry, srz_s, sry_s,
    req, reqz, reqm, reqy, pick, pick_src, pick_slot, reply, mid, got,
    wfull, wt, bcol, ocol, had, hadfull,
    local_sem, sz_send, sz_recv, sy_send, sy_recv, a_send, a_recv, b_send, b_recv,
    qz_send, qz_recv, qy_send, qy_recv, pa_send, pa_recv, pb_send, pb_recv,
    rz_send, rz_recv, ry_send, ry_recv, wx_send, wx_recv, hx_send, hx_recv,
):
    parts = Z * Y * C
    yc, zc = Y * C, Z * C
    queries = src_local.shape[1]
    nodes = embed.shape[1]
    half = embed.shape[0] // 2
    me, xf = lax.axis_index("node"), lax.axis_index("feat")
    z, j = me // yc, me % yc
    y, c = j // C, j % C
    k = z * C + c

    def at_a(jd):
        return (z * yc + jd, xf)

    def at_b(kd):
        return (((kd // C) * Y + y) * C + kd % C, xf)

    def at_z(zd):
        return ((zd * Y + y) * C + c, xf)

    def at_y(yd):
        return ((z * Y + yd) * C + c, xf)

    def at_x(xd):
        return (me, xd)

    def push(src, dst, send, recv, device):
        return pltpu.make_async_remote_copy(
            src_ref=src, dst_ref=dst, send_sem=send, recv_sem=recv, device_id=device, device_id_type=MESH
        )

    def each(lo, hi, body):
        def step(i, carry):
            body(i)
            return carry
        lax.fori_loop(lo, hi, step, 0)

    def zigzag(i, n):
        return jnp.where(i % 2 == 1, (i + 1) // 2, n - i // 2)

    barrier = pltpu.get_barrier_semaphore()

    def greet(device):
        pl.semaphore_signal(barrier, inc=1, device_id=device, device_id_type=MESH)

    ins = [
        pltpu.make_async_copy(src, dst, local_sem.at[4 + n]) for n, (src, dst) in enumerate((
            (embed_in, embed), (send_rows_in, sr_own), (w_in_in, w_in), (tile_rows_in, tile_rows),
            (tile_cols_in, tile_cols), (src_local_in, src_local), (dst_owner_in, dst_owner),
            (dst_local_in, dst_local), (b_in_in, b_in), (w_out_in, w_out),
        ))
    ]
    ins[0].start()
    ins[1].start()
    each(1, yc, lambda e: greet(at_a((j + e) % yc)))
    each(1, zc, lambda e: greet(at_b((k + e) % zc)))
    each(1, X, lambda e: greet(at_x((xf + e) % X)))

    fetch = pltpu.make_async_copy(weight_hbm.at[0], weight, local_sem.at[0])
    for copy in ins[2:]:
        copy.start()
    fetch.start()
    ins[0].wait()
    ins[1].wait()
    for r in range(RB):
        for h in range(2):
            cur0[h, r] = embed[h * half:(h + 1) * half, r * B:(r + 1) * B]

    pl.semaphore_wait(barrier, yc - 1 + zc - 1 + X - 1)

    steps = Z // 2
    near = min(5, Z)
    groups = [(0, near)] + ([(near, Z)] if near < Z else [])
    early = [(d, way) for d in range(1, min(2, steps) + 1) for way in (1, -1)]
    late = [(d, way) for d in range(3, steps + 1) for way in (1, -1)]

    def ring_slot(distance, way):
        return 0 if distance == 0 else 2 * distance - 1 if way == 1 or distance == steps else 2 * distance

    def at_place(near_ref, far_ref, n, rows):
        return near_ref.at[n, rows] if n < near else far_ref.at[n - near, rows]

    def ring_copies(hop, gz, gy, fz, fy, d, way):
        side = 0 if way == 1 else 1
        rows = pl.ds(side * (RB // 2), RB // 2) if d == steps else pl.ds(0, RB)
        start = 0 if d <= 2 else 2
        here, there = ring_slot(start, way), ring_slot(d, way)
        move = way * (d - start)
        return (
            push(at_place(gz, fz, here, rows), at_place(gz, fz, there, rows), sz_send.at[hop, side, d - 1],
                 sz_recv.at[hop, side, d - 1], at_z((z + Z + move) % Z)),
            push(at_place(gy, fy, here, rows), at_place(gy, fy, there, rows), sy_send.at[hop, side, d - 1],
                 sy_recv.at[hop, side, d - 1], at_y((y + Y + move) % Y)),
        )

    def ring_go(bufs, moves):
        for one in moves:
            for copy in ring_copies(*bufs, *one):
                copy.start()

    def ring_end(bufs, moves):
        for one in moves:
            for copy in ring_copies(*bufs, *one):
                copy.wait_recv()

    def deal(hop, group, z_from, y_from, sa, sb, ra, rb):
        lo, hi = groups[group]
        def fill_a(jd, dst):
            for n in range(lo, hi):
                s = (z + Z - zigzag(n, Z)) % Z
                dst[jd, n] = z_from[n - lo, srz_s[s, 0, z * yc + jd]]
        def fill_b(kd, dst):
            for n in range(lo, hi):
                s = (y + Y - zigzag(n, Y)) % Y
                dst[kd, n] = y_from[n - lo, sry_s[s, 0, ((kd // C) * Y + y) * C + kd % C]]
        def go_a(jd):
            fill_a(jd, sa)
            copy_a(hop, group, sa, ra, jd, j).start()
        def go_b(kd):
            fill_b(kd, sb)
            copy_b(hop, group, sb, rb, kd, k).start()
        def ring_step(i):
            i = Y - 1 - i
            if C == 2:
                @pl.when(i == 0)
                def _():
                    go_a(y * C + 1 - c)
                    go_b(z * C + 1 - c)
            @pl.when(i > 0)
            def _():
                yd, zd = (y + zigzag(i, Y)) % Y, (z + zigzag(i, Z)) % Z
                for cd in range(C):
                    go_a(yd * C + cd)
                    go_b(zd * C + cd)
        each(0, Y, ring_step)
        fill_a(j, ra)
        fill_b(k, rb)

    def copy_a(hop, group, sa, ra, there, here):
        lo, hi = groups[group]
        span = pl.ds(lo, hi - lo)
        return push(sa.at[there, span], ra.at[here, span], a_send.at[hop, group, there],
                    a_recv.at[hop, group, here], at_a(there))

    def copy_b(hop, group, sb, rb, there, here):
        lo, hi = groups[group]
        span = pl.ds(lo, hi - lo)
        return push(sb.at[there, span], rb.at[here, span], b_send.at[hop, group, there],
                    b_recv.at[hop, group, here], at_b(there))

    def begin(hop, cur, gz, gy, fz, fy):
        gz[0] = cur[0]
        gy[0] = cur[1]
        ring_go((hop, gz, gy, fz, fy), early)

    def exchange(hop, gz, gy, fz, fy, sa, sb, ra, rb, before_deal):
        bufs = (hop, gz, gy, fz, fy)
        ring_end(bufs, early)
        ring_go(bufs, late)
        before_deal()
        deal(hop, 0, gz, gy, sa, sb, ra, rb)
        if late:
            ring_end(bufs, late)
            deal(hop, 1, fz, fy, sa, sb, ra, rb)

    def combine(hop, cur, sa, sb, ra, rb, nxt):
        def end(group, n):
            zs, ys = (z + Z - zigzag(n, Z)) % Z, (y + Y - zigzag(n, Y)) % Y
            for cs in range(C) if n > 0 else ([1 - c] if C == 2 else []):
                copy_a(hop, group, sa, ra, ys * C + cs, ys * C + cs).wait_recv()
                copy_b(hop, group, sb, rb, zs * C + cs, zs * C + cs).wait_recv()
        def term(s, block):
            product = dot(block, weight[table_s[0, s]], 1, 1)
            total[s] = product + total[table_s[1, s]]
        def pair(s, zi, yi):
            zs, ys = (z + Z - zigzag(zi, Z)) % Z, (y + Y - zigzag(yi, Y)) % Y
            for cs in range(C):
                term(s * C + cs, jnp.concatenate([ra[ys * C + cs, zi], rb[zs * C + cs, yi]], axis=0))
        def corner(n, m):
            pair(n * n + 2 * m, n, m)
            pair(n * n + 2 * m + 1, m, n)
        total[parts] = jnp.zeros(total.shape[1:], F32)
        for r in range(RB):
            block = jnp.concatenate([cur[0, r], cur[1, r]], axis=0)
            own[r] = dot(block, weight[table_s[0, parts + r]], 1, 1)
        ended = set()
        for n in range(Z):
            for group in range(1 if n < near else 2):
                for m in range(n + 1):
                    if (group, m) not in ended:
                        end(group, m)
                        ended.add((group, m))
            def corners(m):
                corner(n, 2 * m)
                corner(n, 2 * m + 1)
            each(0, n // 2, corners)
            if n % 2 == 1:
                corner(n, n - 1)
            pair(n * n + 2 * n, n, n)
        for r in range(RB):
            first = jnp.concatenate([cur0[0, r], cur0[1, r]], axis=0).astype(F32)
            summed = total[table_s[1, parts + r]] + own[r]
            new = ((1.0 - TELEPORT) * summed + TELEPORT * first).astype(BF16)
            nxt[0, r] = new[:half]
            nxt[1, r] = new[half:]


    def rows_z(d):
        push(sr_own, srz.at[z], rz_send.at[d], rz_recv.at[z], at_z((z + d) % Z)).start()
    def rows_y(d):
        push(sr_own, sry.at[y], ry_send.at[d], ry_recv.at[y], at_y((y + d) % Y)).start()
    each(1, Z, rows_z)
    each(1, Y, rows_y)
    srz[z] = sr_own[...]
    sry[y] = sr_own[...]
    begin(0, cur0, gz0, gy0, fz0, fy0)
    ins[2].wait()
    each(1, X, lambda d: push(
        w_in, wfull.at[xf], wx_send.at[d], wx_recv.at[xf], at_x((xf + d) % X)).start())
    wfull[xf] = w_in[...]

    def rows_ready():
        def rows_z_end(d):
            s = (z + d) % Z
            push(sr_own, srz.at[s], rz_send.at[d], rz_recv.at[s], at_z(s)).wait_recv()
        def rows_y_end(d):
            s = (y + d) % Y
            push(sr_own, sry.at[s], ry_send.at[d], ry_recv.at[s], at_y(s)).wait_recv()
        each(1, Z, rows_z_end)
        each(1, Y, rows_y_end)
        rows_copies = [
            pltpu.make_async_copy(srz, srz_s, local_sem.at[2]),
            pltpu.make_async_copy(sry, sry_s, local_sem.at[3]),
        ]
        for copy in rows_copies:
            copy.start()
        for copy in rows_copies:
            copy.wait()
    exchange(0, gz0, gy0, fz0, fy0, sa0, sb0, ra0, rb0, rows_ready)

    for copy in ins[3:]:
        copy.wait()
    slots = cols.shape[1]
    cols[...] = jnp.full(cols.shape, -1, I32)
    tiles = tile_cols.shape[1]
    cols[0:1, 0:tiles] = tile_cols[...]
    cols[8:9, 0:tiles] = tile_rows[...]
    col = cols[0:1, :]
    peer = col - RB
    def ring_place(far, n):
        return jnp.where(far == 0, 0, jnp.where(far <= n // 2, 2 * far - 1, 2 * (n - far)))
    zi = ring_place((z + Z - peer // yc) % Z, Z)
    yi = ring_place((y + Y - peer % yc // C) % Y, Y)
    peer_slot = (jnp.maximum(zi, yi) * jnp.maximum(zi, yi) + 2 * jnp.minimum(zi, yi) + jnp.where(yi > zi, 1, 0)) * C + peer % C
    slot_of = jnp.where(col < 0, -1, jnp.where(col < RB, parts + col, peer_slot))
    hit = (iota((slots, slots), 0) == slot_of).astype(F32).astype(BF16)
    kind = iota((8, slots), 0)
    facts = jnp.where(kind == 0, iota((8, slots), 1), jnp.where(kind == 1, cols[8:9, :], 1))
    found = dot(facts.astype(F32).astype(BF16), hit, 1, 1)
    row_of = jnp.where(found[2:3, :] > 0.5, found[1:2, :], -1.0)
    row_hit = (iota((128, slots), 0).astype(F32) == row_of).astype(F32).astype(BF16)
    same = dot(row_hit, row_hit, 0, 0)
    before = jnp.where(
        (same > 0.5) & (iota((slots, slots), 0) < iota((slots, slots), 1)), iota((slots, slots), 0).astype(F32), -1.0
    )
    last = jnp.max(before, axis=0, keepdims=True)
    table[0:1, :] = jnp.clip(found[0:1, :].astype(I32), 0, tiles - 1)
    table[1:2, :] = jnp.clip(jnp.where(last < 0.0, float(parts), last).astype(I32), 0, parts)
    to_smem = pltpu.make_async_copy(table, table_s, local_sem.at[1])
    to_smem.start()

    owner = dst_owner[...]
    owns = (iota((parts, queries), 0) == owner).astype(F32).astype(BF16)
    alike = dot(owns, owns, 0, 0)
    earlier = iota((queries, queries), 0) < iota((queries, queries), 1)
    rank = jnp.sum(jnp.where(earlier, alike, 0.0), axis=0, keepdims=True).astype(I32)
    place = iota((128, queries), 0) == rank
    high, low = dst_local[...] // 32, dst_local[...] % 32
    ask_high = dot(owns, jnp.where(place, high, 0).astype(F32).astype(BF16), 1, 1)
    ask_low = dot(owns, jnp.where(place, low, 0).astype(F32).astype(BF16), 1, 1)
    req[...] = (ask_high * 32.0 + ask_low).astype(I32).reshape(Z, yc, 128)
    def ask_z(d):
        zd = (z + d) % Z
        push(req.at[zd], reqz.at[z], qz_send.at[d], qz_recv.at[z], at_z(zd)).start()
    each(1, Z, ask_z)
    reqz[z] = req[z]
    fold = CAP // 2
    spot = owner * fold + rank % fold
    for side in range(2):
        spot_side = jnp.where(rank // fold == side, spot, -1)
        pick_slot[side] = (iota(pick_slot.shape[1:], 0) == spot_side).astype(F32).astype(BF16)
    pick_src[...] = (iota(pick_src.shape, 0) == src_local[...]).astype(F32).astype(BF16)

    def w_end(d):
        s = (xf + d) % X
        push(w_in, wfull.at[s], wx_send.at[d], wx_recv.at[s], at_x(s)).wait_recv()
    each(1, X, w_end)
    hidden_units = w_in.shape[1]
    channels = w_in.shape[0]
    for n in range(hidden_units // 128):
        lanes = slice(n * 128, (n + 1) * 128)
        whole = jnp.concatenate([wfull[s, :, lanes] for s in range(X)], axis=0)
        wt[lanes, :] = whole.astype(F32).T.astype(BF16)
        bcol[lanes, :] = jnp.broadcast_to(b_in[0:1, lanes], (128, 128)).T
        ocol[lanes, :] = jnp.broadcast_to(w_out[0:1, lanes], (128, 128)).T

    to_smem.wait()
    fetch.wait()
    combine(0, cur0, sa0, sb0, ra0, rb0, cur1)

    begin(1, cur1, gz1, gy1, fz1, fy1)

    def ask_z_end(d):
        s = (z + d) % Z
        push(req.at[s], reqz.at[s], qz_send.at[d], qz_recv.at[s], at_z(s)).wait_recv()
    each(1, Z, ask_z_end)
    for jd in range(yc):
        reqm[jd] = jnp.concatenate([reqz[s, jd:jd + 1, :] for s in range(Z)], axis=0)
    def ask_y(e):
        jd = (j + e) % yc
        push(reqm.at[jd], reqy.at[j], qy_send.at[e], qy_recv.at[j], at_a(jd)).start()
    each(1, yc, ask_y)
    reqy[j] = reqm[j]

    exchange(1, gz1, gy1, fz1, fy1, sa1, sb1, ra1, rb1, lambda: None)

    def ask_y_end(e):
        s = (j + e) % yc
        push(reqm.at[s], reqy.at[s], qy_send.at[e], qy_recv.at[s], at_a(s)).wait_recv()
    each(1, yc, ask_y_end)
    asked = reqy[...].reshape(parts, 128).astype(F32)
    spread = (iota((parts * fold, parts), 0) // fold == iota((parts * fold, parts), 1)).astype(F32)
    wide = lax.dot_general(
        spread, asked, (((1,), (0,)), ((), ())), precision=lax.Precision.HIGHEST, preferred_element_type=F32
    )
    for side in range(2):
        mine = iota(wide.shape, 1) == iota(wide.shape, 0) % fold + side * fold
        node = jnp.sum(jnp.where(mine, wide, 0.0), axis=1, keepdims=True).astype(I32)
        pick[side] = (iota((parts * fold, nodes), 1) == node).astype(F32).astype(BF16)

    combine(1, cur1, sa1, sb1, ra1, rb1, cur2)
    for r in range(RB):
        for h in range(2):
            out[h * half:(h + 1) * half, r * B:(r + 1) * B] = cur2[h, r]

    final = out[...]
    rows = jnp.concatenate([dot(pick[side], final, 1, 1) for side in range(2)], axis=1)
    reply[...] = rows.reshape(yc, Z, fold, 2 * channels).astype(BF16)
    def reply_a(i):
        jd = (j + i) % yc
        push(reply.at[jd], mid.at[j], pa_send.at[i], pa_recv.at[j], at_a(jd)).start()
    each(1, yc, reply_a)
    mid[j] = reply[j]
    source = dot(final, pick_src[...], 1, 0)
    def reply_a_end(e):
        s = (j + e) % yc
        push(reply.at[s], mid.at[s], pa_send.at[e], pa_recv.at[s], at_a(s)).wait_recv()
    each(1, yc, reply_a_end)
    def reply_z(d):
        zd = (z + d) % Z
        push(mid.at[:, zd], got.at[z], pb_send.at[d], pb_recv.at[z], at_z(zd)).start()
    each(1, Z, reply_z)
    got[z] = mid[:, z]
    def reply_z_end(d):
        s = (z + d) % Z
        push(mid.at[:, s], got.at[s], pb_send.at[d], pb_recv.at[s], at_z(s)).wait_recv()
    each(1, Z, reply_z_end)
    replies = got[...].reshape(parts * fold, 2 * channels)
    target = dot(replies, pick_slot[0], 0, 0)[:channels] + dot(replies, pick_slot[1], 0, 0)[channels:]
    had[...] = (source * target).astype(BF16)
    def had_x(d):
        push(had, hadfull.at[xf], hx_send.at[d], hx_recv.at[xf], at_x((xf + d) % X)).start()
    each(1, X, had_x)
    hadfull[xf] = had[...]
    def had_x_end(d):
        s = (xf + d) % X
        push(had, hadfull.at[s], hx_send.at[d], hx_recv.at[s], at_x(s)).wait_recv()
    each(1, X, had_x_end)
    everything = hadfull[...].reshape(X * channels, queries)
    score = jnp.zeros((8, queries), F32)
    for n in range(hidden_units // 128):
        lanes = slice(n * 128, (n + 1) * 128)
        hidden = dot(wt[lanes, :], everything, 1, 0)
        bias, gain = bcol[lanes, :], ocol[lanes, :]
        if queries > 128:
            bias, gain = (jnp.concatenate([v] * (queries // 128), axis=1) for v in (bias, gain))
        else:
            bias, gain = bias[:, :queries], gain[:, :queries]
        active = jnp.maximum(hidden + bias, 0.0) * gain
        score = score + jnp.sum(active.reshape(16, 8, queries), axis=0)
    scores[...] = jnp.sum(score, axis=0, keepdims=True)

    for hop, gz, gy, fz, fy, sa, sb, ra, rb in (
        (0, gz0, gy0, fz0, fy0, sa0, sb0, ra0, rb0), (1, gz1, gy1, fz1, fy1, sa1, sb1, ra1, rb1)
    ):
        for one in early + late:
            for copy in ring_copies(hop, gz, gy, fz, fy, *one):
                copy.wait_send()
        def left_a(e):
            for group in range(len(groups)):
                copy_a(hop, group, sa, ra, (j + e) % yc, j).wait_send()
        def left_b(e):
            for group in range(len(groups)):
                copy_b(hop, group, sb, rb, (k + e) % zc, k).wait_send()
        each(1, yc, left_a)
        each(1, zc, left_b)
    def left_z(d):
        zd = (z + d) % Z
        push(sr_own, srz.at[z], rz_send.at[d], rz_recv.at[z], at_z(zd)).wait_send()
        push(req.at[zd], reqz.at[z], qz_send.at[d], qz_recv.at[z], at_z(zd)).wait_send()
        push(mid.at[:, zd], got.at[z], pb_send.at[d], pb_recv.at[z], at_z(zd)).wait_send()
    each(1, Z, left_z)
    each(1, Y, lambda d: push(
        sr_own, sry.at[y], ry_send.at[d], ry_recv.at[y], at_y((y + d) % Y)).wait_send())
    def left_y(e):
        jd = (j + e) % yc
        push(reqm.at[jd], reqy.at[j], qy_send.at[e], qy_recv.at[j], at_a(jd)).wait_send()
        push(reply.at[jd], mid.at[j], pa_send.at[e], pa_recv.at[j], at_a(jd)).wait_send()
    each(1, yc, left_y)
    def left_x(d):
        xd = (xf + d) % X
        push(w_in, wfull.at[xf], wx_send.at[d], wx_recv.at[xf], at_x(xd)).wait_send()
        push(had, hadfull.at[xf], hx_send.at[d], hx_recv.at[xf], at_x(xd)).wait_send()
    each(1, X, left_x)


def shards(
    embed, tile_weight, tile_rows, tile_cols, send_rows, src_local, dst_owner, dst_local, w_in, b_in, w_out
):
    parts, yc, zc = Z * Y * C, Y * C, Z * C
    channels, nodes = embed.shape
    half = channels // 2
    queries, hidden = src_local.shape[0], w_in.shape[1]
    tiles = tile_rows.shape[1]
    slots, fold = 256, CAP // 2
    V, S, D = pltpu.VMEM, pltpu.SMEM, pltpu.SemaphoreType.DMA
    cur = [V((2, RB, half, B), BF16)] * 3
    near = [V((min(5, n), RB, half, B), BF16) for n in (Z, Y, Z, Y)]
    near += [V((max(1, n - 5), RB, half, B), BF16) for n in (Z, Y, Z, Y)]
    deal = [V((n, m, half, B), BF16) for n, m in ((yc, Z), (zc, Y))]
    staged = [
        V((channels, nodes), BF16), V((1, tiles), I32), V((1, tiles), I32), V((1, parts), I32),
        V((1, queries), I32), V((1, queries), I32), V((1, queries), I32),
        V((channels, hidden), BF16), V((1, hidden), F32), V((1, hidden), F32),
    ]
    scratch = staged + cur + near + deal * 4 + [
        V((tiles, B, B), BF16), V((parts + 1, channels, B), F32), V((RB, channels, B), F32),
        V((16, slots), I32), V((8, slots), I32), S((8, slots), I32),
        V((Z, 1, parts), I32), V((Y, 1, parts), I32), S((Z, 1, parts), I32), S((Y, 1, parts), I32),
        V((Z, yc, 128), I32), V((Z, yc, 128), I32), V((yc, Z, 128), I32), V((yc, Z, 128), I32),
        V((2, parts * fold, nodes), BF16), V((nodes, queries), BF16), V((2, parts * fold, queries), BF16),
        V((yc, Z, fold, 2 * channels), BF16), V((yc, Z, fold, 2 * channels), BF16), V((Z, yc, fold, 2 * channels), BF16),
        V((X, channels, hidden), BF16), V((hidden, X * channels), BF16), V((hidden, 128), F32), V((hidden, 128), F32),
        V((channels, queries), BF16), V((X, channels, queries), BF16),
        D((14,)), D((HOPS, 2, Z // 2)), D((HOPS, 2, Z // 2)), D((HOPS, 2, Y // 2)), D((HOPS, 2, Y // 2)),
        D((HOPS, 2, yc)), D((HOPS, 2, yc)), D((HOPS, 2, zc)), D((HOPS, 2, zc)),
        D((Z,)), D((Z,)), D((yc,)), D((yc,)), D((yc,)), D((yc,)), D((Z,)), D((Z,)),
        D((Z,)), D((Z,)), D((Y,)), D((Y,)), D((X,)), D((X,)), D((X,)), D((X,)),
    ]
    vmem = pl.BlockSpec(memory_space=pltpu.VMEM)
    propagated, scores = pl.pallas_call(
        kernel,
        out_shape=(
            jax.ShapeDtypeStruct((channels, nodes), BF16),
            jax.ShapeDtypeStruct((1, queries), F32),
        ),
        in_specs=[pl.BlockSpec(memory_space=pl.ANY)] * 11,
        out_specs=(vmem, vmem),
        scratch_shapes=scratch,
        compiler_params=pltpu.CompilerParams(
            collective_id=0, has_side_effects=True, vmem_limit_bytes=56 * 1024 * 1024
        ),
    )(
        embed, tile_weight, tile_rows, tile_cols, send_rows,
        src_local.reshape(1, queries), dst_owner.reshape(1, queries), dst_local.reshape(1, queries),
        w_in, b_in.reshape(1, hidden), w_out.reshape(1, hidden),
    )
    return propagated, scores.reshape(queries)


def solution(mesh):
    placed = (
        P("feat", "node"),
        P("node", None, None, None),
        P("node", None),
        P("node", None),
        P("node", None),
        P("node"),
        P("node", None),
        P("node"),
        P("feat", None),
        P(),
        P(),
    )
    return jax.shard_map(
        shards,
        mesh=mesh,
        in_specs=placed,
        out_specs=(P("feat", "node"), P("node")),
        check_vma=False,
    )
```

```python
import jax
import jax.numpy as jnp
from jax import lax
from jax.experimental import pallas as pl
from jax.experimental.pallas import tpu as pltpu
from jax.sharding import PartitionSpec as P

Z, Y, C, X = 8, 8, 2, 4
RB, B, CAP = 8, 128, 8
HOPS = 2
TELEPORT = 0.1
MESH = pl.DeviceIdType.MESH
F32, BF16, I32 = jnp.float32, jnp.bfloat16, jnp.int32


def dot(left, right, left_dim, right_dim):
    return lax.dot_general(
        left, right, (((left_dim,), (right_dim,)), ((), ())), preferred_element_type=F32
    )


def iota(shape, dim):
    return lax.broadcasted_iota(I32, shape, dim)


def kernel(
    embed_in, weight_hbm, tile_rows_in, tile_cols_in, send_rows_in, src_local_in, dst_owner_in, dst_local_in,
    w_in_in, b_in_in, w_out_in, out, scores,
    embed, tile_rows, tile_cols, sr_own, src_local, dst_owner, dst_local, w_in, b_in, w_out,
    cur0, cur1, cur2, gz0, gy0, gz1, gy1, fz0, fy0, fz1, fy1, sa0, sb0, sa1, sb1, ra0, rb0, ra1, rb1,
    weight, total, own, cols, table, table_s, srz, sry, srz_s, sry_s,
    req, reqz, reqm, reqy, pick, pick_src, pick_slot, reply, mid, got, reply2, mid2, got2,
    wfull, wt, bcol, ocol, had, hadfull,
    local_sem, sz_send, sz_recv, sy_send, sy_recv, a_send, a_recv, b_send, b_recv,
    qz_send, qz_recv, qy_send, qy_recv, pa_send, pa_recv, pb_send, pb_recv,
    pc_send, pc_recv, pd_send, pd_recv,
    rz_send, rz_recv, ry_send, ry_recv, wx_send, wx_recv, hx_send, hx_recv,
):
    parts = Z * Y * C
    yc, zc = Y * C, Z * C
    queries = src_local.shape[1]
    nodes = embed.shape[1]
    half = embed.shape[0] // 2
    me, xf = lax.axis_index("node"), lax.axis_index("feat")
    z, j = me // yc, me % yc
    y, c = j // C, j % C
    k = z * C + c

    def at_a(jd):
        return (z * yc + jd, xf)

    def at_b(kd):
        return (((kd // C) * Y + y) * C + kd % C, xf)

    def at_z(zd):
        return ((zd * Y + y) * C + c, xf)

    def at_y(yd):
        return ((z * Y + yd) * C + c, xf)

    def at_x(xd):
        return (me, xd)

    def push(src, dst, send, recv, device):
        return pltpu.make_async_remote_copy(
            src_ref=src, dst_ref=dst, send_sem=send, recv_sem=recv, device_id=device, device_id_type=MESH
        )

    def each(lo, hi, body):
        def step(i, carry):
            body(i)
            return carry
        lax.fori_loop(lo, hi, step, 0)

    def zigzag(i, n):
        return jnp.where(i % 2 == 1, (i + 1) // 2, n - i // 2)

    barrier = pltpu.get_barrier_semaphore()

    def greet(device):
        pl.semaphore_signal(barrier, inc=1, device_id=device, device_id_type=MESH)

    ins = [
        pltpu.make_async_copy(src, dst, local_sem.at[4 + n]) for n, (src, dst) in enumerate((
            (embed_in, embed), (send_rows_in, sr_own), (w_in_in, w_in), (tile_rows_in, tile_rows),
            (tile_cols_in, tile_cols), (src_local_in, src_local), (dst_owner_in, dst_owner),
            (dst_local_in, dst_local), (b_in_in, b_in), (w_out_in, w_out),
        ))
    ]
    ins[0].start()
    ins[1].start()
    each(1, yc, lambda e: greet(at_a((j + e) % yc)))
    each(1, zc, lambda e: greet(at_b((k + e) % zc)))
    each(1, X, lambda e: greet(at_x((xf + e) % X)))

    fetch = pltpu.make_async_copy(weight_hbm.at[0], weight, local_sem.at[0])
    for copy in ins[2:]:
        copy.start()
    fetch.start()
    ins[0].wait()
    ins[1].wait()
    for r in range(RB):
        for h in range(2):
            cur0[h, r] = embed[h * half:(h + 1) * half, r * B:(r + 1) * B]

    pl.semaphore_wait(barrier, yc - 1 + zc - 1 + X - 1)

    steps = Z // 2
    near = min(5, Z)
    groups = [(0, near)] + ([(near, Z)] if near < Z else [])
    early = [(d, way) for d in range(1, min(2, steps) + 1) for way in (1, -1)]
    late = [(d, way) for d in range(3, steps + 1) for way in (1, -1)]

    def ring_slot(distance, way):
        return 0 if distance == 0 else 2 * distance - 1 if way == 1 or distance == steps else 2 * distance

    def at_place(near_ref, far_ref, n, rows):
        return near_ref.at[n, rows] if n < near else far_ref.at[n - near, rows]

    def ring_copies(hop, gz, gy, fz, fy, d, way):
        side = 0 if way == 1 else 1
        rows = pl.ds(side * (RB // 2), RB // 2) if d == steps else pl.ds(0, RB)
        start = 0 if d <= 2 else 2
        here, there = ring_slot(start, way), ring_slot(d, way)
        move = way * (d - start)
        return (
            push(at_place(gz, fz, here, rows), at_place(gz, fz, there, rows), sz_send.at[hop, side, d - 1],
                 sz_recv.at[hop, side, d - 1], at_z((z + Z + move) % Z)),
            push(at_place(gy, fy, here, rows), at_place(gy, fy, there, rows), sy_send.at[hop, side, d - 1],
                 sy_recv.at[hop, side, d - 1], at_y((y + Y + move) % Y)),
        )

    def ring_go(bufs, moves):
        for one in moves:
            for copy in ring_copies(*bufs, *one):
                copy.start()

    def ring_end(bufs, moves):
        for one in moves:
            for copy in ring_copies(*bufs, *one):
                copy.wait_recv()

    def deal(hop, group, z_from, y_from, sa, sb, ra, rb):
        lo, hi = groups[group]
        def fill_a(jd, dst):
            for n in range(lo, hi):
                s = (z + Z - zigzag(n, Z)) % Z
                dst[jd, n] = z_from[n - lo, srz_s[s, 0, z * yc + jd]]
        def fill_b(kd, dst):
            for n in range(lo, hi):
                s = (y + Y - zigzag(n, Y)) % Y
                dst[kd, n] = y_from[n - lo, sry_s[s, 0, ((kd // C) * Y + y) * C + kd % C]]
        def go_a(jd):
            fill_a(jd, sa)
            copy_a(hop, group, sa, ra, jd, j).start()
        def go_b(kd):
            fill_b(kd, sb)
            copy_b(hop, group, sb, rb, kd, k).start()
        def ring_step(i):
            i = Y - 1 - i
            if C == 2:
                @pl.when(i == 0)
                def _():
                    go_a(y * C + 1 - c)
                    go_b(z * C + 1 - c)
            @pl.when(i > 0)
            def _():
                yd, zd = (y + zigzag(i, Y)) % Y, (z + zigzag(i, Z)) % Z
                for cd in range(C):
                    go_a(yd * C + cd)
                    go_b(zd * C + cd)
        each(0, Y, ring_step)
        fill_a(j, ra)
        fill_b(k, rb)

    def copy_a(hop, group, sa, ra, there, here):
        lo, hi = groups[group]
        span = pl.ds(lo, hi - lo)
        return push(sa.at[there, span], ra.at[here, span], a_send.at[hop, group, there],
                    a_recv.at[hop, group, here], at_a(there))

    def copy_b(hop, group, sb, rb, there, here):
        lo, hi = groups[group]
        span = pl.ds(lo, hi - lo)
        return push(sb.at[there, span], rb.at[here, span], b_send.at[hop, group, there],
                    b_recv.at[hop, group, here], at_b(there))

    def begin(hop, cur, gz, gy, fz, fy):
        gz[0] = cur[0]
        gy[0] = cur[1]
        ring_go((hop, gz, gy, fz, fy), early)

    def exchange(hop, gz, gy, fz, fy, sa, sb, ra, rb, before_deal):
        bufs = (hop, gz, gy, fz, fy)
        ring_end(bufs, early)
        ring_go(bufs, late)
        before_deal()
        deal(hop, 0, gz, gy, sa, sb, ra, rb)
        if late:
            ring_end(bufs, late)
            deal(hop, 1, fz, fy, sa, sb, ra, rb)

    def combine(hop, cur, sa, sb, ra, rb, nxt):
        def end(group, n):
            zs, ys = (z + Z - zigzag(n, Z)) % Z, (y + Y - zigzag(n, Y)) % Y
            for cs in range(C) if n > 0 else ([1 - c] if C == 2 else []):
                copy_a(hop, group, sa, ra, ys * C + cs, ys * C + cs).wait_recv()
                copy_b(hop, group, sb, rb, zs * C + cs, zs * C + cs).wait_recv()
        def term(s, block):
            product = dot(block, weight[table_s[0, s]], 1, 1)
            total[s] = product + total[table_s[1, s]]
        def pair(s, zi, yi):
            zs, ys = (z + Z - zigzag(zi, Z)) % Z, (y + Y - zigzag(yi, Y)) % Y
            for cs in range(C):
                term(s * C + cs, jnp.concatenate([ra[ys * C + cs, zi], rb[zs * C + cs, yi]], axis=0))
        def corner(n, m):
            pair(n * n + 2 * m, n, m)
            pair(n * n + 2 * m + 1, m, n)
        total[parts] = jnp.zeros(total.shape[1:], F32)
        for r in range(RB):
            block = jnp.concatenate([cur[0, r], cur[1, r]], axis=0)
            own[r] = dot(block, weight[table_s[0, parts + r]], 1, 1)
        ended = set()
        for n in range(Z):
            for group in range(1 if n < near else 2):
                for m in range(n + 1):
                    if (group, m) not in ended:
                        end(group, m)
                        ended.add((group, m))
            def corners(m):
                corner(n, 2 * m)
                corner(n, 2 * m + 1)
            each(0, n // 2, corners)
            if n % 2 == 1:
                corner(n, n - 1)
            pair(n * n + 2 * n, n, n)
        for r in range(RB):
            first = jnp.concatenate([cur0[0, r], cur0[1, r]], axis=0).astype(F32)
            summed = total[table_s[1, parts + r]] + own[r]
            new = ((1.0 - TELEPORT) * summed + TELEPORT * first).astype(BF16)
            nxt[0, r] = new[:half]
            nxt[1, r] = new[half:]


    def rows_z(d):
        push(sr_own, srz.at[z], rz_send.at[d], rz_recv.at[z], at_z((z + d) % Z)).start()
    def rows_y(d):
        push(sr_own, sry.at[y], ry_send.at[d], ry_recv.at[y], at_y((y + d) % Y)).start()
    each(1, Z, rows_z)
    each(1, Y, rows_y)
    srz[z] = sr_own[...]
    sry[y] = sr_own[...]
    begin(0, cur0, gz0, gy0, fz0, fy0)
    ins[2].wait()
    each(1, X, lambda d: push(
        w_in, wfull.at[xf], wx_send.at[d], wx_recv.at[xf], at_x((xf + d) % X)).start())
    wfull[xf] = w_in[...]

    def rows_ready():
        def rows_z_end(d):
            s = (z + d) % Z
            push(sr_own, srz.at[s], rz_send.at[d], rz_recv.at[s], at_z(s)).wait_recv()
        def rows_y_end(d):
            s = (y + d) % Y
            push(sr_own, sry.at[s], ry_send.at[d], ry_recv.at[s], at_y(s)).wait_recv()
        each(1, Z, rows_z_end)
        each(1, Y, rows_y_end)
        rows_copies = [
            pltpu.make_async_copy(srz, srz_s, local_sem.at[2]),
            pltpu.make_async_copy(sry, sry_s, local_sem.at[3]),
        ]
        for copy in rows_copies:
            copy.start()
        for copy in rows_copies:
            copy.wait()
    exchange(0, gz0, gy0, fz0, fy0, sa0, sb0, ra0, rb0, rows_ready)

    for copy in ins[3:]:
        copy.wait()
    slots = cols.shape[1]
    cols[...] = jnp.full(cols.shape, -1, I32)
    tiles = tile_cols.shape[1]
    cols[0:1, 0:tiles] = tile_cols[...]
    cols[8:9, 0:tiles] = tile_rows[...]
    col = cols[0:1, :]
    peer = col - RB
    def ring_place(far, n):
        return jnp.where(far == 0, 0, jnp.where(far <= n // 2, 2 * far - 1, 2 * (n - far)))
    zi = ring_place((z + Z - peer // yc) % Z, Z)
    yi = ring_place((y + Y - peer % yc // C) % Y, Y)
    peer_slot = (jnp.maximum(zi, yi) * jnp.maximum(zi, yi) + 2 * jnp.minimum(zi, yi) + jnp.where(yi > zi, 1, 0)) * C + peer % C
    slot_of = jnp.where(col < 0, -1, jnp.where(col < RB, parts + col, peer_slot))
    hit = (iota((slots, slots), 0) == slot_of).astype(F32).astype(BF16)
    kind = iota((8, slots), 0)
    facts = jnp.where(kind == 0, iota((8, slots), 1), jnp.where(kind == 1, cols[8:9, :], 1))
    found = dot(facts.astype(F32).astype(BF16), hit, 1, 1)
    row_of = jnp.where(found[2:3, :] > 0.5, found[1:2, :], -1.0)
    row_hit = (iota((128, slots), 0).astype(F32) == row_of).astype(F32).astype(BF16)
    same = dot(row_hit, row_hit, 0, 0)
    before = jnp.where(
        (same > 0.5) & (iota((slots, slots), 0) < iota((slots, slots), 1)), iota((slots, slots), 0).astype(F32), -1.0
    )
    last = jnp.max(before, axis=0, keepdims=True)
    table[0:1, :] = jnp.clip(found[0:1, :].astype(I32), 0, tiles - 1)
    table[1:2, :] = jnp.clip(jnp.where(last < 0.0, float(parts), last).astype(I32), 0, parts)
    to_smem = pltpu.make_async_copy(table, table_s, local_sem.at[1])
    to_smem.start()

    owner = dst_owner[...]
    owns = (iota((parts, queries), 0) == owner).astype(F32).astype(BF16)
    alike = dot(owns, owns, 0, 0)
    earlier = iota((queries, queries), 0) < iota((queries, queries), 1)
    rank = jnp.sum(jnp.where(earlier, alike, 0.0), axis=0, keepdims=True).astype(I32)
    place = iota((128, queries), 0) == rank
    high, low = dst_local[...] // 32, dst_local[...] % 32
    ask_high = dot(owns, jnp.where(place, high, 0).astype(F32).astype(BF16), 1, 1)
    ask_low = dot(owns, jnp.where(place, low, 0).astype(F32).astype(BF16), 1, 1)
    req[...] = (ask_high * 32.0 + ask_low).astype(I32).reshape(Z, yc, 128)
    def ask_z(d):
        zd = (z + d) % Z
        push(req.at[zd], reqz.at[z], qz_send.at[d], qz_recv.at[z], at_z(zd)).start()
    each(1, Z, ask_z)
    reqz[z] = req[z]
    fold = CAP // 2
    duo = fold // 2
    owner_z, owner_y, owner_c = owner // yc, owner % yc // C, owner % C
    turn = rank % fold
    spot = jnp.where(
        turn < duo, owner * duo + turn,
        parts * duo + (owner_y * zc + owner_z * C + owner_c) * duo + turn - duo,
    )
    for side in range(2):
        spot_side = jnp.where(rank // fold == side, spot, -1)
        pick_slot[side] = (iota(pick_slot.shape[1:], 0) == spot_side).astype(F32).astype(BF16)
    pick_src[...] = (iota(pick_src.shape, 0) == src_local[...]).astype(F32).astype(BF16)

    def w_end(d):
        s = (xf + d) % X
        push(w_in, wfull.at[s], wx_send.at[d], wx_recv.at[s], at_x(s)).wait_recv()
    each(1, X, w_end)
    hidden_units = w_in.shape[1]
    channels = w_in.shape[0]
    for n in range(hidden_units // 128):
        lanes = slice(n * 128, (n + 1) * 128)
        whole = jnp.concatenate([wfull[s, :, lanes] for s in range(X)], axis=0)
        wt[lanes, :] = whole.astype(F32).T.astype(BF16)
        bcol[lanes, :] = jnp.broadcast_to(b_in[0:1, lanes], (128, 128)).T
        ocol[lanes, :] = jnp.broadcast_to(w_out[0:1, lanes], (128, 128)).T

    to_smem.wait()
    fetch.wait()
    combine(0, cur0, sa0, sb0, ra0, rb0, cur1)

    begin(1, cur1, gz1, gy1, fz1, fy1)

    def ask_z_end(d):
        s = (z + d) % Z
        push(req.at[s], reqz.at[s], qz_send.at[d], qz_recv.at[s], at_z(s)).wait_recv()
    each(1, Z, ask_z_end)
    for jd in range(yc):
        reqm[jd] = jnp.concatenate([reqz[s, jd:jd + 1, :] for s in range(Z)], axis=0)
    def ask_y(e):
        jd = (j + e) % yc
        push(reqm.at[jd], reqy.at[j], qy_send.at[e], qy_recv.at[j], at_a(jd)).start()
    each(1, yc, ask_y)
    reqy[j] = reqm[j]

    exchange(1, gz1, gy1, fz1, fy1, sa1, sb1, ra1, rb1, lambda: None)

    def ask_y_end(e):
        s = (j + e) % yc
        push(reqm.at[s], reqy.at[s], qy_send.at[e], qy_recv.at[s], at_a(s)).wait_recv()
    each(1, yc, ask_y_end)
    asked = reqy[...].reshape(parts, 128).astype(F32)
    row = iota((parts * fold, 1), 0)
    row2 = row - parts * duo
    asker = jnp.where(row2 < 0, row // duo, ((row2 // duo % Y) * C + row2 // (duo * Y) % C) * Z + row2 // (duo * Y * C))
    lane = row % duo + jnp.where(row2 < 0, 0, duo)
    spread = (asker == iota((parts * fold, parts), 1)).astype(F32)
    wide = lax.dot_general(
        spread, asked, (((1,), (0,)), ((), ())), precision=lax.Precision.HIGHEST, preferred_element_type=F32
    )
    for side in range(2):
        mine = iota(wide.shape, 1) == lane + side * fold
        node = jnp.sum(jnp.where(mine, wide, 0.0), axis=1, keepdims=True).astype(I32)
        pick[side] = (iota((parts * fold, nodes), 1) == node).astype(F32).astype(BF16)

    combine(1, cur1, sa1, sb1, ra1, rb1, cur2)
    for r in range(RB):
        for h in range(2):
            out[h * half:(h + 1) * half, r * B:(r + 1) * B] = cur2[h, r]

    final = out[...]
    rows = jnp.concatenate([dot(pick[side], final, 1, 1) for side in range(2)], axis=1)
    reply[...] = rows[:parts * duo].reshape(yc, Z, duo, 2 * channels).astype(BF16)
    reply2[...] = rows[parts * duo:].reshape(zc, Y, duo, 2 * channels).astype(BF16)
    def reply_a(i):
        jd = (j + i) % yc
        push(reply.at[jd], mid.at[j], pa_send.at[i], pa_recv.at[j], at_a(jd)).start()
    each(1, yc, reply_a)
    def reply_b(i):
        kd = (k + i) % zc
        push(reply2.at[kd], mid2.at[k], pc_send.at[i], pc_recv.at[k], at_b(kd)).start()
    each(1, zc, reply_b)
    mid[j] = reply[j]
    mid2[k] = reply2[k]
    source = dot(final, pick_src[...], 1, 0)
    def reply_a_end(e):
        s = (j + e) % yc
        push(reply.at[s], mid.at[s], pa_send.at[e], pa_recv.at[s], at_a(s)).wait_recv()
    each(1, yc, reply_a_end)
    def reply_z(d):
        zd = (z + d) % Z
        push(mid.at[:, zd], got.at[z], pb_send.at[d], pb_recv.at[z], at_z(zd)).start()
    each(1, Z, reply_z)
    def reply_b_end(e):
        s = (k + e) % zc
        push(reply2.at[s], mid2.at[s], pc_send.at[e], pc_recv.at[s], at_b(s)).wait_recv()
    each(1, zc, reply_b_end)
    def reply_y(d):
        yd = (y + d) % Y
        push(mid2.at[:, yd], got2.at[y], pd_send.at[d], pd_recv.at[y], at_y(yd)).start()
    each(1, Y, reply_y)
    got[z] = mid[:, z]
    got2[y] = mid2[:, y]
    def reply_z_end(d):
        s = (z + d) % Z
        push(mid.at[:, s], got.at[s], pb_send.at[d], pb_recv.at[s], at_z(s)).wait_recv()
    each(1, Z, reply_z_end)
    def reply_y_end(d):
        s = (y + d) % Y
        push(mid2.at[:, s], got2.at[s], pd_send.at[d], pd_recv.at[s], at_y(s)).wait_recv()
    each(1, Y, reply_y_end)
    replies = jnp.concatenate(
        [half_got[...].reshape(parts * duo, 2 * channels) for half_got in (got, got2)], axis=0
    )
    target = dot(replies, pick_slot[0], 0, 0)[:channels] + dot(replies, pick_slot[1], 0, 0)[channels:]
    had[...] = (source * target).astype(BF16)
    def had_x(d):
        push(had, hadfull.at[xf], hx_send.at[d], hx_recv.at[xf], at_x((xf + d) % X)).start()
    each(1, X, had_x)
    hadfull[xf] = had[...]
    def had_x_end(d):
        s = (xf + d) % X
        push(had, hadfull.at[s], hx_send.at[d], hx_recv.at[s], at_x(s)).wait_recv()
    each(1, X, had_x_end)
    everything = hadfull[...].reshape(X * channels, queries)
    score = jnp.zeros((8, queries), F32)
    for n in range(hidden_units // 128):
        lanes = slice(n * 128, (n + 1) * 128)
        hidden = dot(wt[lanes, :], everything, 1, 0)
        bias, gain = bcol[lanes, :], ocol[lanes, :]
        if queries > 128:
            bias, gain = (jnp.concatenate([v] * (queries // 128), axis=1) for v in (bias, gain))
        else:
            bias, gain = bias[:, :queries], gain[:, :queries]
        active = jnp.maximum(hidden + bias, 0.0) * gain
        score = score + jnp.sum(active.reshape(16, 8, queries), axis=0)
    scores[...] = jnp.sum(score, axis=0, keepdims=True)

    for hop, gz, gy, fz, fy, sa, sb, ra, rb in (
        (0, gz0, gy0, fz0, fy0, sa0, sb0, ra0, rb0), (1, gz1, gy1, fz1, fy1, sa1, sb1, ra1, rb1)
    ):
        for one in early + late:
            for copy in ring_copies(hop, gz, gy, fz, fy, *one):
                copy.wait_send()
        def left_a(e):
            for group in range(len(groups)):
                copy_a(hop, group, sa, ra, (j + e) % yc, j).wait_send()
        def left_b(e):
            for group in range(len(groups)):
                copy_b(hop, group, sb, rb, (k + e) % zc, k).wait_send()
        each(1, yc, left_a)
        each(1, zc, left_b)
    def left_z(d):
        zd = (z + d) % Z
        push(sr_own, srz.at[z], rz_send.at[d], rz_recv.at[z], at_z(zd)).wait_send()
        push(req.at[zd], reqz.at[z], qz_send.at[d], qz_recv.at[z], at_z(zd)).wait_send()
        push(mid.at[:, zd], got.at[z], pb_send.at[d], pb_recv.at[z], at_z(zd)).wait_send()
    each(1, Z, left_z)
    each(1, Y, lambda d: push(
        sr_own, sry.at[y], ry_send.at[d], ry_recv.at[y], at_y((y + d) % Y)).wait_send())
    def left_y(e):
        jd = (j + e) % yc
        push(reqm.at[jd], reqy.at[j], qy_send.at[e], qy_recv.at[j], at_a(jd)).wait_send()
        push(reply.at[jd], mid.at[j], pa_send.at[e], pa_recv.at[j], at_a(jd)).wait_send()
    each(1, yc, left_y)
    each(1, zc, lambda i: push(
        reply2.at[(k + i) % zc], mid2.at[k], pc_send.at[i], pc_recv.at[k], at_b((k + i) % zc)).wait_send())
    each(1, Y, lambda d: push(
        mid2.at[:, (y + d) % Y], got2.at[y], pd_send.at[d], pd_recv.at[y], at_y((y + d) % Y)).wait_send())
    def left_x(d):
        xd = (xf + d) % X
        push(w_in, wfull.at[xf], wx_send.at[d], wx_recv.at[xf], at_x(xd)).wait_send()
        push(had, hadfull.at[xf], hx_send.at[d], hx_recv.at[xf], at_x(xd)).wait_send()
    each(1, X, left_x)


def finish(out_in, scores_in, out, scores):
    out[...] = out_in[...]
    scores[...] = scores_in[...]


def shards(
    embed, tile_weight, tile_rows, tile_cols, send_rows, src_local, dst_owner, dst_local, w_in, b_in, w_out
):
    parts, yc, zc = Z * Y * C, Y * C, Z * C
    channels, nodes = embed.shape
    half = channels // 2
    queries, hidden = src_local.shape[0], w_in.shape[1]
    tiles = tile_rows.shape[1]
    slots, fold, duo = 256, CAP // 2, CAP // 4
    V, S, D = pltpu.VMEM, pltpu.SMEM, pltpu.SemaphoreType.DMA
    cur = [V((2, RB, half, B), BF16)] * 3
    near = [V((min(5, n), RB, half, B), BF16) for n in (Z, Y, Z, Y)]
    near += [V((max(1, n - 5), RB, half, B), BF16) for n in (Z, Y, Z, Y)]
    deal = [V((n, m, half, B), BF16) for n, m in ((yc, Z), (zc, Y))]
    staged = [
        V((channels, nodes), BF16), V((1, tiles), I32), V((1, tiles), I32), V((1, parts), I32),
        V((1, queries), I32), V((1, queries), I32), V((1, queries), I32),
        V((channels, hidden), BF16), V((1, hidden), F32), V((1, hidden), F32),
    ]
    scratch = staged + cur + near + deal * 4 + [
        V((tiles, B, B), BF16), V((parts + 1, channels, B), F32), V((RB, channels, B), F32),
        V((16, slots), I32), V((8, slots), I32), S((8, slots), I32),
        V((Z, 1, parts), I32), V((Y, 1, parts), I32), S((Z, 1, parts), I32), S((Y, 1, parts), I32),
        V((Z, yc, 128), I32), V((Z, yc, 128), I32), V((yc, Z, 128), I32), V((yc, Z, 128), I32),
        V((2, parts * fold, nodes), BF16), V((nodes, queries), BF16), V((2, parts * fold, queries), BF16),
        V((yc, Z, duo, 2 * channels), BF16), V((yc, Z, duo, 2 * channels), BF16), V((Z, yc, duo, 2 * channels), BF16),
        V((zc, Y, duo, 2 * channels), BF16), V((zc, Y, duo, 2 * channels), BF16), V((Y, zc, duo, 2 * channels), BF16),
        V((X, channels, hidden), BF16), V((hidden, X * channels), BF16), V((hidden, 128), F32), V((hidden, 128), F32),
        V((channels, queries), BF16), V((X, channels, queries), BF16),
        D((14,)), D((HOPS, 2, Z // 2)), D((HOPS, 2, Z // 2)), D((HOPS, 2, Y // 2)), D((HOPS, 2, Y // 2)),
        D((HOPS, 2, yc)), D((HOPS, 2, yc)), D((HOPS, 2, zc)), D((HOPS, 2, zc)),
        D((Z,)), D((Z,)), D((yc,)), D((yc,)), D((yc,)), D((yc,)), D((Z,)), D((Z,)),
        D((zc,)), D((zc,)), D((Y,)), D((Y,)),
        D((Z,)), D((Z,)), D((Y,)), D((Y,)), D((X,)), D((X,)), D((X,)), D((X,)),
    ]
    vmem = pl.BlockSpec(memory_space=pltpu.VMEM)
    propagated, scores = pl.pallas_call(
        kernel,
        out_shape=(
            jax.ShapeDtypeStruct((channels, nodes), BF16),
            jax.ShapeDtypeStruct((1, queries), F32),
        ),
        in_specs=[pl.BlockSpec(memory_space=pl.ANY)] * 11,
        out_specs=(vmem, vmem),
        scratch_shapes=scratch,
        compiler_params=pltpu.CompilerParams(
            collective_id=0, has_side_effects=True, vmem_limit_bytes=56 * 1024 * 1024
        ),
    )(
        embed, tile_weight, tile_rows, tile_cols, send_rows,
        src_local.reshape(1, queries), dst_owner.reshape(1, queries), dst_local.reshape(1, queries),
        w_in, b_in.reshape(1, hidden), w_out.reshape(1, hidden),
    )
    propagated, scores = pl.pallas_call(
        finish,
        out_shape=(
            jax.ShapeDtypeStruct((channels, nodes), BF16),
            jax.ShapeDtypeStruct((1, queries), F32),
        ),
        in_specs=[vmem] * 2,
        out_specs=(vmem, vmem),
    )(propagated, scores)
    return propagated, scores.reshape(queries)


def solution(mesh):
    placed = (
        P("feat", "node"),
        P("node", None, None, None),
        P("node", None),
        P("node", None),
        P("node", None),
        P("node"),
        P("node", None),
        P("node"),
        P("feat", None),
        P(),
        P(),
    )
    return jax.shard_map(
        shards,
        mesh=mesh,
        in_specs=placed,
        out_specs=(P("feat", "node"), P("node")),
        check_vma=False,
    )
```

```python
import jax
import jax.numpy as jnp
from jax import lax
from jax.experimental import pallas as pl
from jax.experimental.pallas import tpu as pltpu
from jax.sharding import PartitionSpec as P

Z, Y, C, X = 8, 8, 2, 4
RB, B, CAP = 8, 128, 8
HOPS = 2
TELEPORT = 0.1
MESH = pl.DeviceIdType.MESH
F32, BF16, I32 = jnp.float32, jnp.bfloat16, jnp.int32


def dot(left, right, left_dim, right_dim):
    return lax.dot_general(
        left, right, (((left_dim,), (right_dim,)), ((), ())), preferred_element_type=F32
    )


def iota(shape, dim):
    return lax.broadcasted_iota(I32, shape, dim)


def kernel(
    embed_in, weight_hbm, tile_rows_in, tile_cols_in, send_rows_in, src_local_in, dst_owner_in, dst_local_in,
    w_in_in, b_in_in, w_out_in, out, scores,
    embed, tile_rows, tile_cols, sr_own, src_local, dst_owner, dst_local, w_in, b_in, w_out,
    cur0, cur1, cur2, gz0, gy0, gz1, gy1, fz0, fy0, fz1, fy1, sa0, sb0, sa1, sb1, ra0, rb0, ra1, rb1,
    weight, total, own, cols, table, table_s, srz, sry, srz_s, sry_s,
    req, reqz, reqm, reqy, pick, pick_src, pick_slot, reply, mid, got, reply2, mid2, got2,
    wfull, wt, bcol, ocol, had, hadfull,
    local_sem, sz_send, sz_recv, sy_send, sy_recv, a_send, a_recv, b_send, b_recv,
    qz_send, qz_recv, qy_send, qy_recv, pa_send, pa_recv, pb_send, pb_recv,
    pc_send, pc_recv, pd_send, pd_recv,
    rz_send, rz_recv, ry_send, ry_recv, wx_send, wx_recv, hx_send, hx_recv,
):
    parts = Z * Y * C
    yc, zc = Y * C, Z * C
    queries = src_local.shape[1]
    nodes = embed.shape[1]
    half = embed.shape[0] // 2
    me, xf = lax.axis_index("node"), lax.axis_index("feat")
    z, j = me // yc, me % yc
    y, c = j // C, j % C
    k = z * C + c

    def at_a(jd):
        return (z * yc + jd, xf)

    def at_b(kd):
        return (((kd // C) * Y + y) * C + kd % C, xf)

    def at_z(zd):
        return ((zd * Y + y) * C + c, xf)

    def at_y(yd):
        return ((z * Y + yd) * C + c, xf)

    def at_x(xd):
        return (me, xd)

    def push(src, dst, send, recv, device):
        return pltpu.make_async_remote_copy(
            src_ref=src, dst_ref=dst, send_sem=send, recv_sem=recv, device_id=device, device_id_type=MESH
        )

    def each(lo, hi, body):
        def step(i, carry):
            body(i)
            return carry
        lax.fori_loop(lo, hi, step, 0)

    def zigzag(i, n):
        return jnp.where(i % 2 == 1, (i + 1) // 2, n - i // 2)

    barrier = pltpu.get_barrier_semaphore()

    def greet(device):
        pl.semaphore_signal(barrier, inc=1, device_id=device, device_id_type=MESH)

    ins = [
        pltpu.make_async_copy(src, dst, local_sem.at[4 + n]) for n, (src, dst) in enumerate((
            (embed_in, embed), (send_rows_in, sr_own), (w_in_in, w_in), (tile_rows_in, tile_rows),
            (tile_cols_in, tile_cols), (src_local_in, src_local), (dst_owner_in, dst_owner),
            (dst_local_in, dst_local), (b_in_in, b_in), (w_out_in, w_out),
        ))
    ]
    ins[0].start()
    ins[1].start()
    each(1, yc, lambda e: greet(at_a((j + e) % yc)))
    each(1, zc, lambda e: greet(at_b((k + e) % zc)))
    each(1, X, lambda e: greet(at_x((xf + e) % X)))

    fetch = pltpu.make_async_copy(weight_hbm.at[0], weight, local_sem.at[0])
    for copy in ins[2:]:
        copy.start()
    fetch.start()
    ins[0].wait()
    ins[1].wait()
    for r in range(RB):
        for h in range(2):
            cur0[h, r] = embed[h * half:(h + 1) * half, r * B:(r + 1) * B]

    pl.semaphore_wait(barrier, yc - 1 + zc - 1 + X - 1)

    steps = Z // 2
    near = min(5, Z)
    groups = [(0, near)] + ([(near, Z)] if near < Z else [])
    early = [(d, way) for d in range(1, min(2, steps) + 1) for way in (1, -1)]
    late = [(d, way) for d in range(3, steps + 1) for way in (1, -1)]

    def ring_slot(distance, way):
        return 0 if distance == 0 else 2 * distance - 1 if way == 1 or distance == steps else 2 * distance

    def at_place(near_ref, far_ref, n, rows):
        return near_ref.at[n, rows] if n < near else far_ref.at[n - near, rows]

    def ring_copies(hop, gz, gy, fz, fy, d, way):
        side = 0 if way == 1 else 1
        rows = pl.ds(side * (RB // 2), RB // 2) if d == steps else pl.ds(0, RB)
        start = 0 if d <= 2 else 2
        here, there = ring_slot(start, way), ring_slot(d, way)
        move = way * (d - start)
        return (
            push(at_place(gz, fz, here, rows), at_place(gz, fz, there, rows), sz_send.at[hop, side, d - 1],
                 sz_recv.at[hop, side, d - 1], at_z((z + Z + move) % Z)),
            push(at_place(gy, fy, here, rows), at_place(gy, fy, there, rows), sy_send.at[hop, side, d - 1],
                 sy_recv.at[hop, side, d - 1], at_y((y + Y + move) % Y)),
        )

    def ring_go(bufs, moves):
        for one in moves:
            for copy in ring_copies(*bufs, *one):
                copy.start()

    def ring_end(bufs, moves):
        for one in moves:
            for copy in ring_copies(*bufs, *one):
                copy.wait_recv()

    def deal(hop, group, z_from, y_from, sa, sb, ra, rb):
        lo, hi = groups[group]
        def fill_a(jd, dst):
            for n in range(lo, hi):
                s = (z + Z - zigzag(n, Z)) % Z
                dst[jd, n] = z_from[n - lo, srz_s[s, 0, z * yc + jd]]
        def fill_b(kd, dst):
            for n in range(lo, hi):
                s = (y + Y - zigzag(n, Y)) % Y
                dst[kd, n] = y_from[n - lo, sry_s[s, 0, ((kd // C) * Y + y) * C + kd % C]]
        def go_a(jd):
            fill_a(jd, sa)
            copy_a(hop, group, sa, ra, jd, j).start()
        def go_b(kd):
            fill_b(kd, sb)
            copy_b(hop, group, sb, rb, kd, k).start()
        def ring_step(i):
            i = Y - 1 - i
            if C == 2:
                @pl.when(i == 0)
                def _():
                    go_a(y * C + 1 - c)
                    go_b(z * C + 1 - c)
            @pl.when(i > 0)
            def _():
                yd, zd = (y + zigzag(i, Y)) % Y, (z + zigzag(i, Z)) % Z
                for cd in range(C):
                    go_a(yd * C + cd)
                    go_b(zd * C + cd)
        each(0, Y, ring_step)
        fill_a(j, ra)
        fill_b(k, rb)

    def copy_a(hop, group, sa, ra, there, here):
        lo, hi = groups[group]
        span = pl.ds(lo, hi - lo)
        return push(sa.at[there, span], ra.at[here, span], a_send.at[hop, group, there],
                    a_recv.at[hop, group, here], at_a(there))

    def copy_b(hop, group, sb, rb, there, here):
        lo, hi = groups[group]
        span = pl.ds(lo, hi - lo)
        return push(sb.at[there, span], rb.at[here, span], b_send.at[hop, group, there],
                    b_recv.at[hop, group, here], at_b(there))

    def begin(hop, cur, gz, gy, fz, fy):
        gz[0] = cur[0]
        gy[0] = cur[1]
        ring_go((hop, gz, gy, fz, fy), early)

    def exchange(hop, gz, gy, fz, fy, sa, sb, ra, rb, before_deal):
        bufs = (hop, gz, gy, fz, fy)
        ring_end(bufs, early)
        ring_go(bufs, late)
        before_deal()
        deal(hop, 0, gz, gy, sa, sb, ra, rb)
        if late:
            ring_end(bufs, late)
            deal(hop, 1, fz, fy, sa, sb, ra, rb)

    def drain(hop, gz, gy, fz, fy, sa, sb, ra, rb):
        for one in early + late:
            for copy in ring_copies(hop, gz, gy, fz, fy, *one):
                copy.wait_send()
        def left_a(e):
            for group in range(len(groups)):
                copy_a(hop, group, sa, ra, (j + e) % yc, j).wait_send()
        def left_b(e):
            for group in range(len(groups)):
                copy_b(hop, group, sb, rb, (k + e) % zc, k).wait_send()
        each(1, yc, left_a)
        each(1, zc, left_b)

    def combine(hop, cur, sa, sb, ra, rb, nxt):
        def end(group, n):
            zs, ys = (z + Z - zigzag(n, Z)) % Z, (y + Y - zigzag(n, Y)) % Y
            for cs in range(C) if n > 0 else ([1 - c] if C == 2 else []):
                copy_a(hop, group, sa, ra, ys * C + cs, ys * C + cs).wait_recv()
                copy_b(hop, group, sb, rb, zs * C + cs, zs * C + cs).wait_recv()
        def term(s, block):
            product = dot(block, weight[table_s[0, s]], 1, 1)
            total[s] = product + total[table_s[1, s]]
        def pair(s, zi, yi):
            zs, ys = (z + Z - zigzag(zi, Z)) % Z, (y + Y - zigzag(yi, Y)) % Y
            for cs in range(C):
                term(s * C + cs, jnp.concatenate([ra[ys * C + cs, zi], rb[zs * C + cs, yi]], axis=0))
        def corner(n, m):
            pair(n * n + 2 * m, n, m)
            pair(n * n + 2 * m + 1, m, n)
        total[parts] = jnp.zeros(total.shape[1:], F32)
        for r in range(RB):
            block = jnp.concatenate([cur[0, r], cur[1, r]], axis=0)
            own[r] = dot(block, weight[table_s[0, parts + r]], 1, 1)
        ended = set()
        for n in range(Z):
            for group in range(1 if n < near else 2):
                for m in range(n + 1):
                    if (group, m) not in ended:
                        end(group, m)
                        ended.add((group, m))
            def corners(m):
                corner(n, 2 * m)
                corner(n, 2 * m + 1)
            each(0, n // 2, corners)
            if n % 2 == 1:
                corner(n, n - 1)
            pair(n * n + 2 * n, n, n)
        for r in range(RB):
            first = jnp.concatenate([cur0[0, r], cur0[1, r]], axis=0).astype(F32)
            summed = total[table_s[1, parts + r]] + own[r]
            new = ((1.0 - TELEPORT) * summed + TELEPORT * first).astype(BF16)
            nxt[0, r] = new[:half]
            nxt[1, r] = new[half:]


    def rows_z(d):
        push(sr_own, srz.at[z], rz_send.at[d], rz_recv.at[z], at_z((z + d) % Z)).start()
    def rows_y(d):
        push(sr_own, sry.at[y], ry_send.at[d], ry_recv.at[y], at_y((y + d) % Y)).start()
    each(1, Z, rows_z)
    each(1, Y, rows_y)
    srz[z] = sr_own[...]
    sry[y] = sr_own[...]
    begin(0, cur0, gz0, gy0, fz0, fy0)
    ins[2].wait()
    each(1, X, lambda d: push(
        w_in, wfull.at[xf], wx_send.at[d], wx_recv.at[xf], at_x((xf + d) % X)).start())
    wfull[xf] = w_in[...]

    def rows_ready():
        def rows_z_end(d):
            s = (z + d) % Z
            push(sr_own, srz.at[s], rz_send.at[d], rz_recv.at[s], at_z(s)).wait_recv()
        def rows_y_end(d):
            s = (y + d) % Y
            push(sr_own, sry.at[s], ry_send.at[d], ry_recv.at[s], at_y(s)).wait_recv()
        each(1, Z, rows_z_end)
        each(1, Y, rows_y_end)
        rows_copies = [
            pltpu.make_async_copy(srz, srz_s, local_sem.at[2]),
            pltpu.make_async_copy(sry, sry_s, local_sem.at[3]),
        ]
        for copy in rows_copies:
            copy.start()
        for copy in rows_copies:
            copy.wait()
    exchange(0, gz0, gy0, fz0, fy0, sa0, sb0, ra0, rb0, rows_ready)

    for copy in ins[3:]:
        copy.wait()
    slots = cols.shape[1]
    cols[...] = jnp.full(cols.shape, -1, I32)
    tiles = tile_cols.shape[1]
    cols[0:1, 0:tiles] = tile_cols[...]
    cols[8:9, 0:tiles] = tile_rows[...]
    col = cols[0:1, :]
    peer = col - RB
    def ring_place(far, n):
        return jnp.where(far == 0, 0, jnp.where(far <= n // 2, 2 * far - 1, 2 * (n - far)))
    zi = ring_place((z + Z - peer // yc) % Z, Z)
    yi = ring_place((y + Y - peer % yc // C) % Y, Y)
    peer_slot = (jnp.maximum(zi, yi) * jnp.maximum(zi, yi) + 2 * jnp.minimum(zi, yi) + jnp.where(yi > zi, 1, 0)) * C + peer % C
    slot_of = jnp.where(col < 0, -1, jnp.where(col < RB, parts + col, peer_slot))
    hit = (iota((slots, slots), 0) == slot_of).astype(F32).astype(BF16)
    kind = iota((8, slots), 0)
    facts = jnp.where(kind == 0, iota((8, slots), 1), jnp.where(kind == 1, cols[8:9, :], 1))
    found = dot(facts.astype(F32).astype(BF16), hit, 1, 1)
    row_of = jnp.where(found[2:3, :] > 0.5, found[1:2, :], -1.0)
    row_hit = (iota((128, slots), 0).astype(F32) == row_of).astype(F32).astype(BF16)
    same = dot(row_hit, row_hit, 0, 0)
    before = jnp.where(
        (same > 0.5) & (iota((slots, slots), 0) < iota((slots, slots), 1)), iota((slots, slots), 0).astype(F32), -1.0
    )
    last = jnp.max(before, axis=0, keepdims=True)
    table[0:1, :] = jnp.clip(found[0:1, :].astype(I32), 0, tiles - 1)
    table[1:2, :] = jnp.clip(jnp.where(last < 0.0, float(parts), last).astype(I32), 0, parts)
    to_smem = pltpu.make_async_copy(table, table_s, local_sem.at[1])
    to_smem.start()

    owner = dst_owner[...]
    owns = (iota((parts, queries), 0) == owner).astype(F32).astype(BF16)
    alike = dot(owns, owns, 0, 0)
    earlier = iota((queries, queries), 0) < iota((queries, queries), 1)
    rank = jnp.sum(jnp.where(earlier, alike, 0.0), axis=0, keepdims=True).astype(I32)
    place = iota((128, queries), 0) == rank
    high, low = dst_local[...] // 32, dst_local[...] % 32
    ask_high = dot(owns, jnp.where(place, high, 0).astype(F32).astype(BF16), 1, 1)
    ask_low = dot(owns, jnp.where(place, low, 0).astype(F32).astype(BF16), 1, 1)
    req[...] = (ask_high * 32.0 + ask_low).astype(I32).reshape(Z, yc, 128)
    def ask_z(d):
        zd = (z + d) % Z
        push(req.at[zd], reqz.at[z], qz_send.at[d], qz_recv.at[z], at_z(zd)).start()
    each(1, Z, ask_z)
    reqz[z] = req[z]
    fold = CAP // 2
    duo = fold // 2
    owner_z, owner_y, owner_c = owner // yc, owner % yc // C, owner % C
    turn = rank % fold
    spot = jnp.where(
        turn < duo, owner * duo + turn,
        parts * duo + (owner_y * zc + owner_z * C + owner_c) * duo + turn - duo,
    )
    for side in range(2):
        spot_side = jnp.where(rank // fold == side, spot, -1)
        pick_slot[side] = (iota(pick_slot.shape[1:], 0) == spot_side).astype(F32).astype(BF16)
    pick_src[...] = (iota(pick_src.shape, 0) == src_local[...]).astype(F32).astype(BF16)

    def w_end(d):
        s = (xf + d) % X
        push(w_in, wfull.at[s], wx_send.at[d], wx_recv.at[s], at_x(s)).wait_recv()
    each(1, X, w_end)
    hidden_units = w_in.shape[1]
    channels = w_in.shape[0]
    for n in range(hidden_units // 128):
        lanes = slice(n * 128, (n + 1) * 128)
        whole = jnp.concatenate([wfull[s, :, lanes] for s in range(X)], axis=0)
        wt[lanes, :] = whole.astype(F32).T.astype(BF16)
        bcol[lanes, :] = jnp.broadcast_to(b_in[0:1, lanes], (128, 128)).T
        ocol[lanes, :] = jnp.broadcast_to(w_out[0:1, lanes], (128, 128)).T

    to_smem.wait()
    fetch.wait()
    combine(0, cur0, sa0, sb0, ra0, rb0, cur1)

    begin(1, cur1, gz1, gy1, fz1, fy1)

    def ask_z_end(d):
        s = (z + d) % Z
        push(req.at[s], reqz.at[s], qz_send.at[d], qz_recv.at[s], at_z(s)).wait_recv()
    each(1, Z, ask_z_end)
    for jd in range(yc):
        reqm[jd] = jnp.concatenate([reqz[s, jd:jd + 1, :] for s in range(Z)], axis=0)
    def ask_y(e):
        jd = (j + e) % yc
        push(reqm.at[jd], reqy.at[j], qy_send.at[e], qy_recv.at[j], at_a(jd)).start()
    each(1, yc, ask_y)
    reqy[j] = reqm[j]

    exchange(1, gz1, gy1, fz1, fy1, sa1, sb1, ra1, rb1, lambda: None)

    drain(0, gz0, gy0, fz0, fy0, sa0, sb0, ra0, rb0)

    def ask_y_end(e):
        s = (j + e) % yc
        push(reqm.at[s], reqy.at[s], qy_send.at[e], qy_recv.at[s], at_a(s)).wait_recv()
    each(1, yc, ask_y_end)
    asked = reqy[...].reshape(parts, 128).astype(F32)
    row = iota((parts * fold, 1), 0)
    row2 = row - parts * duo
    asker = jnp.where(row2 < 0, row // duo, ((row2 // duo % Y) * C + row2 // (duo * Y) % C) * Z + row2 // (duo * Y * C))
    lane = row % duo + jnp.where(row2 < 0, 0, duo)
    spread = (asker == iota((parts * fold, parts), 1)).astype(F32)
    wide = lax.dot_general(
        spread, asked, (((1,), (0,)), ((), ())), precision=lax.Precision.HIGHEST, preferred_element_type=F32
    )
    for side in range(2):
        mine = iota(wide.shape, 1) == lane + side * fold
        node = jnp.sum(jnp.where(mine, wide, 0.0), axis=1, keepdims=True).astype(I32)
        pick[side] = (iota((parts * fold, nodes), 1) == node).astype(F32).astype(BF16)

    combine(1, cur1, sa1, sb1, ra1, rb1, cur2)
    for r in range(RB):
        for h in range(2):
            out[h * half:(h + 1) * half, r * B:(r + 1) * B] = cur2[h, r]

    final = out[...]
    rows = jnp.concatenate([dot(pick[side], final, 1, 1) for side in range(2)], axis=1)
    reply[...] = rows[:parts * duo].reshape(yc, Z, duo, 2 * channels).astype(BF16)
    reply2[...] = rows[parts * duo:].reshape(zc, Y, duo, 2 * channels).astype(BF16)
    def reply_a(i):
        jd = (j + i) % yc
        push(reply.at[jd], mid.at[j], pa_send.at[i], pa_recv.at[j], at_a(jd)).start()
    each(1, yc, reply_a)
    def reply_b(i):
        kd = (k + i) % zc
        push(reply2.at[kd], mid2.at[k], pc_send.at[i], pc_recv.at[k], at_b(kd)).start()
    each(1, zc, reply_b)
    mid[j] = reply[j]
    mid2[k] = reply2[k]
    source = dot(final, pick_src[...], 1, 0)
    drain(1, gz1, gy1, fz1, fy1, sa1, sb1, ra1, rb1)
    def reply_a_end(e):
        s = (j + e) % yc
        push(reply.at[s], mid.at[s], pa_send.at[e], pa_recv.at[s], at_a(s)).wait_recv()
    each(1, yc, reply_a_end)
    def reply_z(d):
        zd = (z + d) % Z
        push(mid.at[:, zd], got.at[z], pb_send.at[d], pb_recv.at[z], at_z(zd)).start()
    each(1, Z, reply_z)
    def reply_b_end(e):
        s = (k + e) % zc
        push(reply2.at[s], mid2.at[s], pc_send.at[e], pc_recv.at[s], at_b(s)).wait_recv()
    each(1, zc, reply_b_end)
    def reply_y(d):
        yd = (y + d) % Y
        push(mid2.at[:, yd], got2.at[y], pd_send.at[d], pd_recv.at[y], at_y(yd)).start()
    each(1, Y, reply_y)
    got[z] = mid[:, z]
    got2[y] = mid2[:, y]
    def reply_z_end(d):
        s = (z + d) % Z
        push(mid.at[:, s], got.at[s], pb_send.at[d], pb_recv.at[s], at_z(s)).wait_recv()
    each(1, Z, reply_z_end)
    def reply_y_end(d):
        s = (y + d) % Y
        push(mid2.at[:, s], got2.at[s], pd_send.at[d], pd_recv.at[s], at_y(s)).wait_recv()
    each(1, Y, reply_y_end)
    replies = jnp.concatenate(
        [half_got[...].reshape(parts * duo, 2 * channels) for half_got in (got, got2)], axis=0
    )
    target = dot(replies, pick_slot[0], 0, 0)[:channels] + dot(replies, pick_slot[1], 0, 0)[channels:]
    had[...] = (source * target).astype(BF16)
    def had_x(d):
        push(had, hadfull.at[xf], hx_send.at[d], hx_recv.at[xf], at_x((xf + d) % X)).start()
    each(1, X, had_x)
    hadfull[xf] = had[...]
    def had_x_end(d):
        s = (xf + d) % X
        push(had, hadfull.at[s], hx_send.at[d], hx_recv.at[s], at_x(s)).wait_recv()
    each(1, X, had_x_end)
    everything = hadfull[...].reshape(X * channels, queries)
    score = jnp.zeros((8, queries), F32)
    for n in range(hidden_units // 128):
        lanes = slice(n * 128, (n + 1) * 128)
        hidden = dot(wt[lanes, :], everything, 1, 0)
        bias, gain = bcol[lanes, :], ocol[lanes, :]
        if queries > 128:
            bias, gain = (jnp.concatenate([v] * (queries // 128), axis=1) for v in (bias, gain))
        else:
            bias, gain = bias[:, :queries], gain[:, :queries]
        active = jnp.maximum(hidden + bias, 0.0) * gain
        score = score + jnp.sum(active.reshape(16, 8, queries), axis=0)
    scores[...] = jnp.sum(score, axis=0, keepdims=True)

    def left_z(d):
        zd = (z + d) % Z
        push(sr_own, srz.at[z], rz_send.at[d], rz_recv.at[z], at_z(zd)).wait_send()
        push(req.at[zd], reqz.at[z], qz_send.at[d], qz_recv.at[z], at_z(zd)).wait_send()
        push(mid.at[:, zd], got.at[z], pb_send.at[d], pb_recv.at[z], at_z(zd)).wait_send()
    each(1, Z, left_z)
    each(1, Y, lambda d: push(
        sr_own, sry.at[y], ry_send.at[d], ry_recv.at[y], at_y((y + d) % Y)).wait_send())
    def left_y(e):
        jd = (j + e) % yc
        push(reqm.at[jd], reqy.at[j], qy_send.at[e], qy_recv.at[j], at_a(jd)).wait_send()
        push(reply.at[jd], mid.at[j], pa_send.at[e], pa_recv.at[j], at_a(jd)).wait_send()
    each(1, yc, left_y)
    each(1, zc, lambda i: push(
        reply2.at[(k + i) % zc], mid2.at[k], pc_send.at[i], pc_recv.at[k], at_b((k + i) % zc)).wait_send())
    each(1, Y, lambda d: push(
        mid2.at[:, (y + d) % Y], got2.at[y], pd_send.at[d], pd_recv.at[y], at_y((y + d) % Y)).wait_send())
    def left_x(d):
        xd = (xf + d) % X
        push(w_in, wfull.at[xf], wx_send.at[d], wx_recv.at[xf], at_x(xd)).wait_send()
        push(had, hadfull.at[xf], hx_send.at[d], hx_recv.at[xf], at_x(xd)).wait_send()
    each(1, X, left_x)


def finish(out_in, scores_in, out, scores):
    out[...] = out_in[...]
    scores[...] = scores_in[...]


def shards(
    embed, tile_weight, tile_rows, tile_cols, send_rows, src_local, dst_owner, dst_local, w_in, b_in, w_out
):
    parts, yc, zc = Z * Y * C, Y * C, Z * C
    channels, nodes = embed.shape
    half = channels // 2
    queries, hidden = src_local.shape[0], w_in.shape[1]
    tiles = tile_rows.shape[1]
    slots, fold, duo = 256, CAP // 2, CAP // 4
    V, S, D = pltpu.VMEM, pltpu.SMEM, pltpu.SemaphoreType.DMA
    cur = [V((2, RB, half, B), BF16)] * 3
    near = [V((min(5, n), RB, half, B), BF16) for n in (Z, Y, Z, Y)]
    near += [V((max(1, n - 5), RB, half, B), BF16) for n in (Z, Y, Z, Y)]
    deal = [V((n, m, half, B), BF16) for n, m in ((yc, Z), (zc, Y))]
    staged = [
        V((channels, nodes), BF16), V((1, tiles), I32), V((1, tiles), I32), V((1, parts), I32),
        V((1, queries), I32), V((1, queries), I32), V((1, queries), I32),
        V((channels, hidden), BF16), V((1, hidden), F32), V((1, hidden), F32),
    ]
    scratch = staged + cur + near + deal * 4 + [
        V((tiles, B, B), BF16), V((parts + 1, channels, B), F32), V((RB, channels, B), F32),
        V((16, slots), I32), V((8, slots), I32), S((8, slots), I32),
        V((Z, 1, parts), I32), V((Y, 1, parts), I32), S((Z, 1, parts), I32), S((Y, 1, parts), I32),
        V((Z, yc, 128), I32), V((Z, yc, 128), I32), V((yc, Z, 128), I32), V((yc, Z, 128), I32),
        V((2, parts * fold, nodes), BF16), V((nodes, queries), BF16), V((2, parts * fold, queries), BF16),
        V((yc, Z, duo, 2 * channels), BF16), V((yc, Z, duo, 2 * channels), BF16), V((Z, yc, duo, 2 * channels), BF16),
        V((zc, Y, duo, 2 * channels), BF16), V((zc, Y, duo, 2 * channels), BF16), V((Y, zc, duo, 2 * channels), BF16),
        V((X, channels, hidden), BF16), V((hidden, X * channels), BF16), V((hidden, 128), F32), V((hidden, 128), F32),
        V((channels, queries), BF16), V((X, channels, queries), BF16),
        D((14,)), D((HOPS, 2, Z // 2)), D((HOPS, 2, Z // 2)), D((HOPS, 2, Y // 2)), D((HOPS, 2, Y // 2)),
        D((HOPS, 2, yc)), D((HOPS, 2, yc)), D((HOPS, 2, zc)), D((HOPS, 2, zc)),
        D((Z,)), D((Z,)), D((yc,)), D((yc,)), D((yc,)), D((yc,)), D((Z,)), D((Z,)),
        D((zc,)), D((zc,)), D((Y,)), D((Y,)),
        D((Z,)), D((Z,)), D((Y,)), D((Y,)), D((X,)), D((X,)), D((X,)), D((X,)),
    ]
    vmem = pl.BlockSpec(memory_space=pltpu.VMEM)
    propagated, scores = pl.pallas_call(
        kernel,
        out_shape=(
            jax.ShapeDtypeStruct((channels, nodes), BF16),
            jax.ShapeDtypeStruct((1, queries), F32),
        ),
        in_specs=[pl.BlockSpec(memory_space=pl.ANY)] * 11,
        out_specs=(vmem, vmem),
        scratch_shapes=scratch,
        compiler_params=pltpu.CompilerParams(
            collective_id=0, has_side_effects=True, vmem_limit_bytes=56 * 1024 * 1024
        ),
    )(
        embed, tile_weight, tile_rows, tile_cols, send_rows,
        src_local.reshape(1, queries), dst_owner.reshape(1, queries), dst_local.reshape(1, queries),
        w_in, b_in.reshape(1, hidden), w_out.reshape(1, hidden),
    )
    propagated, scores = pl.pallas_call(
        finish,
        out_shape=(
            jax.ShapeDtypeStruct((channels, nodes), BF16),
            jax.ShapeDtypeStruct((1, queries), F32),
        ),
        in_specs=[vmem] * 2,
        out_specs=(vmem, vmem),
    )(propagated, scores)
    return propagated, scores.reshape(queries)


def solution(mesh):
    placed = (
        P("feat", "node"),
        P("node", None, None, None),
        P("node", None),
        P("node", None),
        P("node", None),
        P("node"),
        P("node", None),
        P("node"),
        P("feat", None),
        P(),
        P(),
    )
    return jax.shard_map(
        shards,
        mesh=mesh,
        in_specs=placed,
        out_specs=(P("feat", "node"), P("node")),
        check_vma=False,
    )
```
